256 devices in a mesh: blk: 32 (over x, z_lo, core), head: 8 (over y, z_hi).
Axes of the slice: x: 4, y: 4, z: 8 (z_hi: 2, z_lo: 4; z = z_hi * 4 + z_lo), core: 2. Of those that a mesh axis runs over, the one named last changes fastest.
Arguments:
- query: bfloat16 [8, 16384, 128], P('head', 'blk'), may hold values from -12 to 12
- key: bfloat16 [16384, 128], P('blk'), may hold values from -6 to 6
- value: bfloat16 [16384, 128], P('blk'), may hold values from -6 to 6
- output: bfloat16 [8, 16384, 128], P('head', 'blk'), may hold values from -6 to 6
- out_grad: bfloat16 [8, 16384, 128], P('head', 'blk'), may hold values from -6 to 6
- lse: float32 [8, 16384], P('head', 'blk'), may hold values from 5 to 14
- block_order: int32 [64], replicated, may hold values from 0 to 63, as said below
Outputs:
- grad_query: float32 [8, 16384, 128], P('head', 'blk')
- grad_key: float32 [16384, 128], P(('blk', 'head'))
- grad_value: float32 [16384, 128], P(('blk', 'head'))
The draws below stay inside these ranges and needn't reach their ends.
Inputs may be any that keep to these rules, and one draw needn't show every extreme that they name: A permutation of 0 to 63; the storage block j, rows j * 256 to (j + 1) * 256 - 1, holds the sequence block block_order[j].
All inputs are finite; a program needn't handle non-finite values.
Results may differ from the reference program's by a relative error of at most 0.0036.
Values may be sent and summed in bfloat16 or wider, within the bound.
A program may use at most 64 MiB of HBM per device.

```python
import jax
import jax.numpy as jnp
from jax import lax

DH = 128
BLOCK = 256
NBLOCKS = 64
SEQ = 16384
HEADS = 8


def block_table(key):
    return jax.random.permutation(jax.random.fold_in(key, 11), NBLOCKS).astype(jnp.int32)


def draw_block_order(key, part):
    return block_table(key)


def draw_lse(key, part):
    table = block_table(key)
    rows = jnp.arange(SEQ, dtype=jnp.int32)
    pos = table[rows // BLOCK] * BLOCK + rows % BLOCK
    base = jnp.log(pos.astype(jnp.float32) + 64.0) + 2.0
    noise_key = jax.random.fold_in(key, 23)
    noise = jax.random.uniform(noise_key, (HEADS, SEQ), jnp.float32, -0.5, 0.5)
    return base[None, :] + noise


def steps_of(own_key, shape, cuts, low, high):
    loudness, own = 1.0, jax.random.fold_in(own_key, 6)
    for position, blocks in cuts:
        steps = jnp.exp(jax.random.uniform(jax.random.fold_in(own, position), (blocks,), jnp.float32, low / len(cuts), high / len(cuts)))
        loudness = loudness * jnp.repeat(steps, shape[position] // blocks).reshape([-1 if axis == position else 1 for axis in range(len(shape))])
    return loudness


def bell_draw(rng, dims, deviation, most, shards=(), kind=jnp.bfloat16):
    drawn = deviation * jax.random.normal(rng, dims, jnp.float32)
    if shards:
        drawn = drawn * steps_of(rng, dims, shards, -0.22, 0.18)
    return jnp.clip(drawn, -most, most).astype(kind)


def setup_inputs(seed: int = 0) -> dict:
    key_of = jax.random.split(jax.random.key(seed), 8)
    query = bell_draw(key_of[0], (HEADS, SEQ, DH), 2.0, 12.0, ((0, 8), (1, 32)))
    key = bell_draw(key_of[1], (SEQ, DH), 1.0, 6.0, ((0, 32),))
    value = bell_draw(key_of[2], (SEQ, DH), 1.0, 6.0, ((0, 32),))
    output = bell_draw(key_of[3], (HEADS, SEQ, DH), 1.0, 6.0, ((0, 8), (1, 32)))
    out_grad = bell_draw(key_of[4], (HEADS, SEQ, DH), 1.0, 6.0, ((0, 8), (1, 32)))
    lse = draw_lse(jax.random.fold_in(key_of[7], 71), 0)
    block_order = draw_block_order(jax.random.fold_in(key_of[7], 71), 0)
    return dict(query=query, key=key, value=value, output=output, out_grad=out_grad, lse=lse, block_order=block_order)


def positions(block_order):
    rows = jnp.arange(SEQ, dtype=jnp.int32)
    return block_order[rows // BLOCK].astype(jnp.int32) * BLOCK + rows % BLOCK


def reference(query, key, value, output, out_grad, lse, block_order):
    scale = DH ** -0.5
    pos = positions(block_order)
    delta = jnp.sum(out_grad.astype(jnp.float32) * output.astype(jnp.float32), axis=-1)
    key_wide = key.astype(jnp.float32)
    value_wide = value.astype(jnp.float32)
    count = SEQ // BLOCK

    def step(carry, index):
        grad_k, grad_v = carry
        start = index * BLOCK
        q_rows = lax.dynamic_slice_in_dim(query, start, BLOCK, 1).astype(jnp.float32)
        g_rows = lax.dynamic_slice_in_dim(out_grad, start, BLOCK, 1).astype(jnp.float32)
        l_rows = lax.dynamic_slice_in_dim(lse, start, BLOCK, 1)
        d_rows = lax.dynamic_slice_in_dim(delta, start, BLOCK, 1)
        q_pos = lax.dynamic_slice_in_dim(pos, start, BLOCK, 0)
        scores = jnp.einsum("hqd,kd->hqk", q_rows, key_wide) * scale
        live = q_pos[:, None] >= pos[None, :]
        probs = jnp.where(live[None], jnp.exp(scores - l_rows[..., None]), 0.0)
        probs_low = probs.astype(jnp.bfloat16).astype(jnp.float32)
        dprobs = jnp.einsum("hqd,kd->hqk", g_rows, value_wide)
        dscores = (probs * (dprobs - d_rows[..., None])).astype(jnp.bfloat16).astype(jnp.float32)
        grad_q = jnp.einsum("hqk,kd->hqd", dscores, key_wide) * scale
        grad_k = grad_k + jnp.einsum("hqk,hqd->kd", dscores, q_rows) * scale
        grad_v = grad_v + jnp.einsum("hqk,hqd->kd", probs_low, g_rows)
        return (grad_k, grad_v), grad_q

    empty = jnp.zeros((SEQ, DH), jnp.float32)
    (grad_key, grad_value), blocks = lax.scan(step, (empty, empty), jnp.arange(count, dtype=jnp.int32))
    grad_query = jnp.transpose(blocks, (1, 0, 2, 3)).reshape(HEADS, SEQ, DH)
    return grad_query, grad_key, grad_value
```

```python
import jax
import jax.numpy as jnp
from jax import lax
from jax.experimental import pallas as pl
from jax.experimental.pallas import tpu as pltpu
from jax.sharding import PartitionSpec as P

F32 = jnp.float32
BF16 = jnp.bfloat16
MESH = pl.DeviceIdType.MESH
LOG2E = 1.4426950408889634
DEAD = 1.0e9
X, Z, C, Y = 4, 4, 2, 4
RING = 8


def dot(left, right, left_dim, right_dim):
    return lax.dot_general(
        left, right, (((left_dim,), (right_dim,)), ((), ())), preferred_element_type=F32
    )


def kernel(
    q_hbm, k_hbm, v_hbm, o_hbm, g_hbm, l_hbm, order,
    dq_out, dk_out, dv_out,
    qb, gb, sb, kb, vb, ob, lb,
    dq_acc, dk_acc, dv_acc, core_in, x_out, x_in,
    y_out, y_own, y_in, z_out, z_own, z_in,
    load_sem, send_sem, q_sem, g_sem, s_sem, k_sem, v_sem, core_sem, x_sem, y_sem, z_sem,
):
    rows, feat = k_hbm.shape
    half = rows // 2
    scale = feat ** -0.5
    blk = lax.axis_index("blk")
    head = lax.axis_index("head")
    core = blk % C
    zlo = (blk // C) % Z
    x = blk // (C * Z)
    zhi = head % 2
    y = head // 2
    ring = zhi * Z + zlo

    def at(dx=0, dc=0):
        return {"blk": (((x + dx) % X) * Z + zlo) * C + (core + dc) % C, "head": head}

    def at_y(dy):
        return {"blk": blk, "head": ((y + dy) % Y) * 2 + zhi}

    def at_ring(dz):
        there = (ring + dz) % RING
        return {"blk": (x * Z + there % Z) * C + core, "head": y * 2 + there // Z}

    greeted = (
        [at(dc=1)] + [at(dx=i) for i in (1, 2, 3)] + [at_y(i) for i in (1, 2, 3)]
        + [at_ring(i) for i in range(1, RING)]
    )
    barrier = pltpu.get_barrier_semaphore()
    for device in greeted:
        pl.semaphore_signal(barrier, inc=1, device_id=device, device_id_type=MESH)

    loads = []
    own = pl.ds(0, rows)
    for i, (src, dst) in enumerate((
        (g_hbm.at[0], gb.at[0, own]), (o_hbm.at[0], ob), (l_hbm, lb),
        (q_hbm.at[0], qb.at[0, own]), (k_hbm, kb.at[0]), (v_hbm, vb.at[0]),
    )):
        loads.append(pltpu.make_async_copy(src, dst, load_sem.at[i]))
        loads[-1].start()

    sends = []

    def remote(src, dst, recv, device):
        copy = pltpu.make_async_remote_copy(
            src_ref=src, dst_ref=dst, send_sem=send_sem.at[len(sends)], recv_sem=recv,
            device_id=device, device_id_type=MESH,
        )
        sends.append(copy)
        return copy

    def landing(dst, recv):
        return pltpu.make_async_remote_copy(
            src_ref=dst, dst_ref=dst, send_sem=send_sem.at[0], recv_sem=recv,
            device_id=at(dc=1), device_id_type=MESH,
        )

    def slot(buf, s):
        return buf.at[s // 2, pl.ds((s % 2) * rows, rows)]

    def stat(s):
        return sb.at[s // 2, :, pl.ds((s % 2) * rows, rows)]

    def pass_slot(src, dst, device):
        return [
            remote(slot(qb, src), slot(qb, dst), q_sem.at[dst], device),
            remote(slot(gb, src), slot(gb, dst), g_sem.at[dst], device),
            remote(stat(src), stat(dst), s_sem.at[dst], device),
        ]

    def wait_slot(s):
        landing(slot(qb, s), q_sem.at[s]).wait_recv()
        landing(slot(gb, s), g_sem.at[s]).wait_recv()
        landing(stat(s), s_sem.at[s]).wait_recv()

    to_core = pass_slot(0, 1, at(dc=1))
    to_right = pass_slot(0, 3, at(dx=1))
    to_left = pass_slot(0, 2, at(dx=3))
    keys_out = [
        remote(kb.at[0], kb.at[2], k_sem.at[2], at_ring(1)),
        remote(kb.at[0], kb.at[1], k_sem.at[1], at_ring(7)),
        remote(vb.at[0], vb.at[2], v_sem.at[2], at_ring(1)),
        remote(vb.at[0], vb.at[1], v_sem.at[1], at_ring(7)),
    ]
    forward = pass_slot(2, 4, at(dc=1)) + pass_slot(3, 5, at(dc=1))
    relay_x = [
        remote(slot(qb, 2), slot(qb, 6), q_sem.at[6], at(dx=3)),
        remote(slot(gb, 3), slot(gb, 6), g_sem.at[6], at(dx=1)),
        remote(stat(2), stat(6), s_sem.at[6], at(dx=3)),
    ]
    relay_z = [
        remote(kb.at[1], kb.at[3], k_sem.at[3], at_ring(7)),
        remote(vb.at[2], vb.at[3], v_sem.at[3], at_ring(1)),
    ]
    forward_far = pass_slot(6, 7, at(dc=1))
    core_pairs = {7: 6, 4: 2, 5: 3, 1: 0}
    core_index = {7: 0, 4: 1, 5: 2, 1: 3}
    dq_core = {
        s: remote(dq_acc.at[s], core_in.at[i], core_sem.at[i], at(dc=1))
        for s, i in core_index.items()
    }
    dq_x = {i: remote(x_out.at[i - 1], x_in.at[i - 1], x_sem.at[i - 1], at(dx=i)) for i in (1, 2, 3)}
    kv_y = {
        (r, i): remote(y_out.at[r, (y + i) % Y], y_in.at[r, i - 1], y_sem.at[r, i - 1], at_y(i))
        for r in range(Z) for i in (1, 2, 3)
    }
    turn_of = (0, 1, 3, 2)
    kv_z = {}
    for r in range(Z):
        for i in (turn_of[r], turn_of[r] + Z):
            if i:
                there = (ring + i) % RING
                kv_z[r, i] = remote(
                    z_out.at[r, there // Z], z_in.at[i - 1], z_sem.at[i - 1], at_ring(i)
                )

    def start(copies):
        for copy in copies:
            copy.start()

    loads[0].wait()
    loads[1].wait()
    loads[2].wait()
    delta = jnp.sum(jnp.transpose(gb[0, own].astype(F32) * ob[...].astype(F32)), axis=0, keepdims=True)
    sb[0, 0:1, own] = lb[...] * LOG2E
    sb[0, 1:2, own] = delta
    for i in (3, 4, 5):
        loads[i].wait()
    pl.semaphore_wait(barrier, len(greeted))

    start(to_core[:2])
    start([to_right[0], to_left[0], to_right[1], to_left[1]])
    start(keys_out)

    dq_acc[...] = jnp.zeros_like(dq_acc)
    dk_acc[...] = jnp.zeros_like(dk_acc)
    dv_acc[...] = jnp.zeros_like(dv_acc)
    start([to_core[2], to_right[2], to_left[2]])

    def chunk_blocks(dx, dc, dz):
        c = ((x + dx) % X * Z + (zlo + dz) % Z) * C + (core + dc) % C
        return order[2 * c], order[2 * c + 1]

    def grads(keys, vals, q_rows, g_rows, probs, d_row):
        dprobs = dot(vals, g_rows, 1, 1)
        dscores = (probs * (dprobs - d_row)).astype(BF16)
        dv_acc[...] += dot(probs.astype(BF16), g_rows, 1, 0)
        dk_acc[...] += dot(dscores, q_rows, 1, 0)
        return dot(keys, dscores, 0, 0)

    def biased(l_row, q_blocks, k_block):
        parts = []
        for i, q_block in enumerate(q_blocks):
            dead = jnp.where(q_block > k_block, 0.0, DEAD)
            parts.append(l_row[:, i * half : (i + 1) * half] + dead)
        return jnp.concatenate(parts, axis=1)

    def tile(r, p, first, count, q_blocks, k_blocks):
        cols = pl.ds(first * rows, count * rows)
        keys, vals = kb[r], vb[r]
        q_rows, g_rows = qb[p, cols], gb[p, cols]
        l_row, d_row = sb[p, 0:1, cols], sb[p, 1:2, cols]
        lows = jnp.stack([biased(l_row, q_blocks, b) for b in k_blocks])
        scores = dot(keys, q_rows, 1, 1).reshape(2, half, count * rows)
        probs = jnp.exp2(scores * (scale * LOG2E) - lows).reshape(rows, count * rows)
        part = grads(keys, vals, q_rows, g_rows, probs, d_row)
        for i in range(count):
            dq_acc[2 * p + first + i] += part[:, i * rows : (i + 1) * rows]

    own_blocks = chunk_blocks(0, 0, 0)
    q_rows, g_rows = qb[0, own], gb[0, own]
    at_row = lax.broadcasted_iota(jnp.int32, (rows, rows), 0)
    at_col = lax.broadcasted_iota(jnp.int32, (rows, rows), 1)
    k_pos = jnp.where(at_row < half, own_blocks[0], own_blocks[1]) * half + at_row % half
    q_pos = jnp.where(at_col < half, own_blocks[0], own_blocks[1]) * half + at_col % half
    scores = dot(kb[0], q_rows, 1, 1)
    probs = jnp.where(
        q_pos >= k_pos, jnp.exp2(scores * (scale * LOG2E) - sb[0, 0:1, own]), 0.0
    )
    dq_acc[0] += grads(kb[0], vb[0], q_rows, g_rows, probs, sb[0, 1:2, own])

    wait_slot(1)
    tile(0, 0, 1, 1, chunk_blocks(0, 1, 0), own_blocks)

    quarter = rows // Y
    eighth = quarter // 2

    def stage_row(r):
        y_out[r, :, :, :feat] = dk_acc[...].astype(BF16).reshape(Y, quarter, feat)
        y_out[r, :, :, feat:] = dv_acc[...].astype(BF16).reshape(Y, quarter, feat)
        mine = pl.ds(y * quarter, quarter)
        y_own[r, :, :feat] = dk_acc[mine]
        y_own[r, :, feat:] = dv_acc[mine]
        dk_acc[...] = jnp.zeros_like(dk_acc)
        dv_acc[...] = jnp.zeros_like(dv_acc)

    def sum_y(r):
        total = y_own[r]
        for i in range(Y - 1):
            landing(y_in.at[r, i], y_sem.at[r, i]).wait_recv()
            total = total + y_in[r, i].astype(F32)
        total = total.reshape(2, eighth, 2 * feat)
        z_out[r] = total.astype(BF16)
        if r == 0:
            y_own[0] = total.reshape(quarter, 2 * feat)
            z_own[...] = y_own[0, pl.ds(zhi * eighth, eighth)]

    def send_y(r):
        start([kv_y[r, i] for i in (2, 1, 3)])

    def send_z(r):
        start([copy for (row, _), copy in kv_z.items() if row == r])

    def join_core(s, index):
        i = core_index[s]
        landing(core_in.at[i], core_sem.at[i]).wait_recv()
        x_out[index] = (dq_acc[core_pairs[s]] + core_in[i]).astype(BF16)

    def step(t, carry):
        r = t // 4
        p = t % 4 + (r // 3) * (3 - 2 * (t % 4))

        @pl.when(t == 1)
        def _():
            wait_slot(2)
            wait_slot(3)
            start(forward)
            start(relay_x)

        @pl.when(t == 2)
        def _():
            for i in (1, 2):
                landing(kb.at[i], k_sem.at[i]).wait_recv()
                landing(vb.at[i], v_sem.at[i]).wait_recv()
            start(relay_z)
            wait_slot(4)
            wait_slot(5)

        @pl.when(t == 3)
        def _():
            wait_slot(6)
            start(forward_far)
            wait_slot(7)

        @pl.when(t == 12)
        def _():
            landing(kb.at[3], k_sem.at[3]).wait_recv()
            landing(vb.at[3], v_sem.at[3]).wait_recv()

        near = (p + 1) // 2
        q_blocks = chunk_blocks(near, p // 2 - p // 3, 0) + chunk_blocks(
            4 - near, 1 - p % 2 + p // 3, 0
        )
        k_blocks = chunk_blocks(0, 0, r + r // 2 - 2 * (r // 3))
        tile(r, p, 0, 2, q_blocks, k_blocks)

        for r_done in range(3):
            @pl.when(t == 4 * r_done + 4)
            def _():
                send_y(r_done)
                if r_done >= 1:
                    send_z(r_done - 1)

        for r_done in range(4):
            @pl.when(t == 4 * r_done + 3)
            def _():
                if r_done >= 1:
                    sum_y(r_done - 1)
                stage_row(r_done)

        @pl.when(t == 12)
        def _():
            dq_core[7].start()

        @pl.when(t == 13)
        def _():
            dq_core[4].start()
            dq_core[5].start()
            join_core(7, 1)

        @pl.when(t == 14)
        def _():
            dq_x[2].start()
            join_core(4, 0)
            join_core(5, 2)

        @pl.when(t == 15)
        def _():
            dq_x[1].start()
            dq_x[3].start()
            dq_core[1].start()

        return carry

    lax.fori_loop(1, 16, step, 0)

    send_y(3)
    send_z(2)
    landing(core_in.at[3], core_sem.at[3]).wait_recv()
    total = dq_acc[0] + core_in[3]
    for i in range(X - 1):
        landing(x_in.at[i], x_sem.at[i]).wait_recv()
        total = total + x_in[i].astype(F32)
    dq_out[0] = jnp.transpose(total * scale)
    sum_y(3)
    send_z(3)
    total = z_own[...]
    for i in (4, 1, 5, 3, 7, 2, 6):
        landing(z_in.at[i - 1], z_sem.at[i - 1]).wait_recv()
        total = total + z_in[i - 1].astype(F32)
    dk_out[...] = total[:, :feat] * scale
    dv_out[...] = total[:, feat:]
    for copy in sends:
        copy.wait_send()


def on_device(query, key, value, output, out_grad, lse, block_order):
    rows, feat = key.shape
    quarter, eighth = rows // Y, rows // RING
    any_space = pl.BlockSpec(memory_space=pl.ANY)
    vmem = pl.BlockSpec(memory_space=pltpu.VMEM)
    dma = pltpu.SemaphoreType.DMA
    return pl.pallas_call(
        kernel,
        out_shape=(
            jax.ShapeDtypeStruct((1, rows, feat), F32),
            jax.ShapeDtypeStruct((eighth, feat), F32),
            jax.ShapeDtypeStruct((eighth, feat), F32),
        ),
        in_specs=[any_space] * 6 + [pl.BlockSpec(memory_space=pltpu.SMEM)],
        out_specs=(vmem, vmem, vmem),
        scratch_shapes=[
            pltpu.VMEM((4, 2 * rows, feat), BF16),
            pltpu.VMEM((4, 2 * rows, feat), BF16),
            pltpu.VMEM((4, 2, 2 * rows), F32),
            pltpu.VMEM((Z, rows, feat), BF16),
            pltpu.VMEM((Z, rows, feat), BF16),
            pltpu.VMEM((rows, feat), BF16),
            pltpu.VMEM((1, rows), F32),
            pltpu.VMEM((8, feat, rows), F32),
            pltpu.VMEM((rows, feat), F32),
            pltpu.VMEM((rows, feat), F32),
            pltpu.VMEM((4, feat, rows), F32),
            pltpu.VMEM((X - 1, feat, rows), BF16),
            pltpu.VMEM((X - 1, feat, rows), BF16),
            pltpu.VMEM((Z, Y, quarter, 2 * feat), BF16),
            pltpu.VMEM((Z, quarter, 2 * feat), F32),
            pltpu.VMEM((Z, Y - 1, quarter, 2 * feat), BF16),
            pltpu.VMEM((Z, 2, eighth, 2 * feat), BF16),
            pltpu.VMEM((eighth, 2 * feat), F32),
            pltpu.VMEM((RING - 1, eighth, 2 * feat), BF16),
            dma((6,)),
            dma((64,)),
            dma((8,)),
            dma((8,)),
            dma((8,)),
            dma((Z,)),
            dma((Z,)),
            dma((4,)),
            dma((X - 1,)),
            dma((Z, Y - 1)),
            dma((RING - 1,)),
        ],
        compiler_params=pltpu.CompilerParams(
            collective_id=0, has_side_effects=True, vmem_limit_bytes=48 << 20
        ),
        name="attention_backward",
    )(query, key, value, output, out_grad, lse, block_order)


def solution(mesh):
    in_specs = (
        P("head", "blk", None),
        P("blk", None),
        P("blk", None),
        P("head", "blk", None),
        P("head", "blk", None),
        P("head", "blk"),
        P(),
    )
    out_specs = (P("head", "blk", None), P(("blk", "head"), None), P(("blk", "head"), None))
    return jax.shard_map(
        on_device, mesh=mesh, in_specs=in_specs, out_specs=out_specs, check_vma=False
    )
```

```python
import jax
import jax.numpy as jnp
from jax import lax
from jax.experimental import pallas as pl
from jax.experimental.pallas import tpu as pltpu
from jax.sharding import PartitionSpec as P

F32 = jnp.float32
BF16 = jnp.bfloat16
MESH = pl.DeviceIdType.MESH
LOG2E = 1.4426950408889634
DEAD = 1.0e9
PAIR = (0, 0, 1, 1, 0, 2, 2, 1, 3, 3, 2, 3, 3, 2, 1, 0)
KEYS = (0, 1, 0, 1, 2, 0, 1, 2, 0, 1, 2, 2, 3, 3, 3, 3)
X, Z, C, Y = 4, 4, 2, 4
RING = 8


def dot(left, right, left_dim, right_dim):
    return lax.dot_general(
        left, right, (((left_dim,), (right_dim,)), ((), ())), preferred_element_type=F32
    )


def kernel(
    q_hbm, k_hbm, v_hbm, o_hbm, g_hbm, l_hbm, order,
    dq_out, dkv_out,
    qb, gb, sb, kb, vb, ob, lb,
    dq_acc, dk_acc, dv_acc, core_in, x_out, x_in,
    y_out, y_own, y_in, z_out, z_in, dq_rows,
    load_sem, send_sem, q_sem, g_sem, s_sem, k_sem, v_sem, core_sem, x_sem, y_sem, z_sem,
):
    rows, feat = ob.shape
    half, piece = rows // 2, rows // RING
    scale = feat ** -0.5
    blk = lax.axis_index("blk")
    head = lax.axis_index("head")
    core = blk % C
    zlo = (blk // C) % Z
    x = blk // (C * Z)
    zhi = head % 2
    y = head // 2
    ring = zhi * Z + zlo

    def at(dx=0, dc=0):
        return {"blk": (((x + dx) % X) * Z + zlo) * C + (core + dc) % C, "head": head}

    def at_y(dy):
        return {"blk": blk, "head": ((y + dy) % Y) * 2 + zhi}

    def at_ring(dz):
        there = (ring + dz) % RING
        return {"blk": (x * Z + there % Z) * C + core, "head": y * 2 + there // Z}

    greeted = (
        [at(dc=1)] + [at(dx=i) for i in (1, 2, 3)] + [at_y(i) for i in (1, 2, 3)]
        + [at_ring(i) for i in range(1, RING)]
    )
    barrier = pltpu.get_barrier_semaphore()
    for device in greeted:
        pl.semaphore_signal(barrier, inc=1, device_id=device, device_id_type=MESH)

    loads = []
    own = pl.ds(0, rows)
    for src, dst in (
        (g_hbm.at[0], gb.at[0, own]), (o_hbm.at[0], ob), (l_hbm, lb), (q_hbm.at[0], qb.at[0, own]),
        (k_hbm.at[:, 0], kb.at[0, 0]), (v_hbm.at[:, 0], vb.at[0, 0]),
        (k_hbm.at[:, 1], kb.at[0, 1]), (v_hbm.at[:, 1], vb.at[0, 1]),
    ):
        loads.append(pltpu.make_async_copy(src, dst, load_sem.at[len(loads)]))
        loads[-1].start()

    sends = []

    def remote(src, dst, recv, device):
        copy = pltpu.make_async_remote_copy(
            src_ref=src, dst_ref=dst, send_sem=send_sem.at[len(sends)], recv_sem=recv,
            device_id=device, device_id_type=MESH,
        )
        sends.append(copy)
        return copy

    def landed(dst, recv):
        pltpu.make_async_remote_copy(
            src_ref=dst, dst_ref=dst, send_sem=send_sem.at[0], recv_sem=recv,
            device_id=at(dc=1), device_id_type=MESH,
        ).wait_recv()

    def start(copies):
        for copy in copies:
            copy.start()

    def part(buf, place):
        p, first, count = place
        return buf.at[p, pl.ds(first, count)]

    def stat(place):
        p, first, count = place
        return sb.at[p, :, pl.ds(first, count)]

    def pass_q(src, dst, i, device):
        return remote(part(qb, src), part(qb, dst), q_sem.at[i], device)

    def pass_g(src, dst, i, device):
        return remote(part(gb, src), part(gb, dst), g_sem.at[i], device)

    def pass_s(src, dst, i, device):
        return remote(stat(src), stat(dst), s_sem.at[i], device)

    def pass_all(src, dst, i, device):
        return [f(src, dst, i, device) for f in (pass_q, pass_g, pass_s)]

    def got(place, i):
        landed(part(qb, place), q_sem.at[i])
        landed(part(gb, place), g_sem.at[i])
        landed(stat(place), s_sem.at[i])

    def got_keys(r, h):
        landed(kb.at[r, h], k_sem.at[r, h])
        landed(vb.at[r, h], v_sem.at[r, h])

    to_core = pass_all((0, 0, rows), (0, rows, rows), 0, at(dc=1))
    waves, keys_out, forward, relay_x, relay_z = [], [], [], [], []
    for w in (0, 1):
        mine, p, i = (0, w * half, half), 1 + w, 3 * w + 1
        right = pass_all(mine, (p, half, half), i + 1, at(dx=1))
        left = pass_all(mine, (p, 0, half), i, at(dx=3))
        waves.append((right, left))
        keys_out.append([
            remote(buf.at[0, w], buf.at[p, h], sem.at[p, h], at_ring(dz))
            for buf, sem in ((kb, k_sem), (vb, v_sem)) for h, dz in ((1, 1), (0, 7))
        ])
        forward.append(pass_all((p, 0, rows), (p, rows, rows), i + 2, at(dc=1)))
        far = (3, w * half, half)
        relay_x.append([
            pass_q((p, 0, half), far, 7 + w, at(dx=3)),
            pass_g((p, half, half), far, 7 + w, at(dx=1)),
            pass_s((p, 0, half), far, 7 + w, at(dx=3)),
        ])
        relay_z.append([
            remote(buf.at[p, w], buf.at[3, w], sem.at[3, w], at_ring((7, 1)[w]))
            for buf, sem in ((kb, k_sem), (vb, v_sem))
        ])
    forward_far = pass_all((3, 0, rows), (3, rows, rows), 9, at(dc=1))
    dq_core = [remote(dq_acc.at[p, 1], core_in.at[p], core_sem.at[p], at(dc=1)) for p in range(4)]
    dq_x = [None] + [
        [remote(x_out.at[w, i], x_in.at[2 * i, w], x_sem.at[2 * i, w], at(dx=(1, 3)[i])) for i in (0, 1)]
        for w in (0, 1)
    ] + [[remote(x_out.at[2, w], x_in.at[1, w], x_sem.at[1, w], at(dx=2)) for w in (0, 1)]]
    kv_y = [
        [remote(y_out.at[r, (y + i) % Y], y_in.at[r, i - 1], y_sem.at[r, i - 1], at_y(i)) for i in (2, 1, 3)]
        for r in range(4)
    ]
    kv_z = [[remote(z_out.at[0, 1 - zhi], z_in.at[Z - 1], z_sem.at[Z - 1], at_ring(Z))]]
    for r, targets in ((1, ((1, 0), (3, 0))), (2, ((1, 1), (3, 1))), (3, ((2, 0), (2, 1)))):
        kv_z.append([])
        for h, (dz, side) in enumerate(targets):
            ahead = (side * Z + (zlo + dz) % Z - ring + RING) % RING
            kv_z[r].append(
                remote(z_out.at[r, h], z_in.at[ahead - 1], z_sem.at[ahead - 1], at_ring(ahead))
            )

    for i in (0, 1, 2):
        loads[i].wait()
    delta = jnp.sum(jnp.transpose(gb[0, own].astype(F32) * ob[...].astype(F32)), axis=0, keepdims=True)
    sb[0, 0:1, own] = lb[...] * LOG2E
    sb[0, 1:2, own] = delta
    for i in range(3, 8):
        loads[i].wait()
    pl.semaphore_wait(barrier, len(greeted))

    start(to_core[:2])
    for w in (0, 1):
        right, left = waves[w]
        start([right[0], left[0], right[1], left[1]])
        start(keys_out[w])
        if w == 0:
            dq_acc[...] = jnp.zeros_like(dq_acc)
            start([to_core[2]])
        start([right[2], left[2]])
    dk_acc[...] = jnp.zeros_like(dk_acc)
    dv_acc[...] = jnp.zeros_like(dv_acc)

    def block(dx, dc, dz, b):
        return order[2 * (((x + dx) % X * Z + (zlo + dz) % Z) * C + (core + dc) % C) + b]

    def grads(r, keys, vals, q_rows, g_rows, probs, d_row):
        dprobs = dot(vals, g_rows, 1, 1)
        dscores = (probs * (dprobs - d_row)).astype(BF16)
        dv_acc[r] += dot(probs.astype(BF16), g_rows, 1, 0).reshape(2, Y, piece, feat)
        dk_acc[r] += dot(dscores, q_rows, 1, 0).reshape(2, Y, piece, feat)
        return dot(keys, dscores, 0, 0)

    def biased(l_row, q_blocks, k_block):
        parts = []
        for i, q_block in enumerate(q_blocks):
            dead = jnp.where(q_block > k_block, 0.0, DEAD)
            parts.append(l_row[:, i * half : (i + 1) * half] + dead)
        return jnp.concatenate(parts, axis=1)

    def tile(r, p, first, count, q_blocks, k_blocks):
        cols = pl.ds(first * rows, count * rows)
        keys, vals = kb[r].reshape(rows, feat), vb[r].reshape(rows, feat)
        q_rows, g_rows = qb[p, cols], gb[p, cols]
        l_row, d_row = sb[p, 0:1, cols], sb[p, 1:2, cols]
        lows = jnp.stack([biased(l_row, q_blocks, b) for b in k_blocks])
        scores = dot(keys, q_rows, 1, 1).reshape(4, half // 2, count * rows)
        probs = jnp.exp2(scores * (scale * LOG2E) - lows).reshape(rows, count * rows)
        part_q = grads(r, keys, vals, q_rows, g_rows, probs, d_row)
        for i in range(count):
            dq_acc[p, first + i] += part_q[:, i * rows : (i + 1) * rows]

    own_blocks = [block(0, 0, 0, b) for b in (0, 1)]
    q_rows, g_rows = qb[0, own], gb[0, own]
    at_row = lax.broadcasted_iota(jnp.int32, (rows, 1), 0)
    at_col = lax.broadcasted_iota(jnp.int32, (1, rows), 1)
    quarter = at_row % half // piece
    k_off = quarter % 2 * (2 * piece) + at_row // half * piece + at_row % piece
    k_pos = jnp.where(quarter < 2, own_blocks[0], own_blocks[1]) * half + k_off
    q_pos = jnp.where(at_col < half, own_blocks[0], own_blocks[1]) * half + at_col % half
    keys, vals = kb[0].reshape(rows, feat), vb[0].reshape(rows, feat)
    scores = dot(keys, q_rows, 1, 1)
    probs = jnp.where(
        q_pos >= k_pos, jnp.exp2(scores * (scale * LOG2E) - sb[0, 0:1, own]), 0.0
    )
    dq_acc[0, 0] += grads(0, keys, vals, q_rows, g_rows, probs, sb[0, 1:2, own])

    got((0, rows, rows), 0)
    tile(0, 0, 1, 1, [block(0, 1, 0, b) for b in (0, 1)], own_blocks * 2)

    def stage_row(r):
        for h in (0, 1):
            y_out[r, :, h, :, :feat] = dk_acc[r, h].astype(BF16)
            y_out[r, :, h, :, feat:] = dv_acc[r, h].astype(BF16)
            y_own[r, h, :, :feat] = dk_acc[r, h, y]
            y_own[r, h, :, feat:] = dv_acc[r, h, y]

    def sum_y(r):
        total = y_own[r]
        for i in range(Y - 1):
            landed(y_in.at[r, i], y_sem.at[r, i])
            total = total + y_in[r, i].astype(F32)
        z_out[r] = total.astype(BF16)
        if r == 0:
            y_own[0] = total

    def join_core(p):
        landed(core_in.at[p], core_sem.at[p])
        total = (dq_acc[p, 0] + core_in[p]).astype(BF16)
        x_out[p - 1, 0] = total[:, :half]
        x_out[p - 1, 1] = total[:, half:]

    before = {
        1: lambda: (
            got((1, 0, half), 1), got((1, half, half), 2), start(forward[0]), start(relay_x[0]),
            got_keys(1, 0), start(relay_z[0]), got_keys(1, 1),
        ),
        2: lambda: got((1, rows, rows), 3),
        3: lambda: (
            got((2, 0, half), 4), got((2, half, half), 5), start(forward[1]), start(relay_x[1]),
        ),
        4: lambda: (got_keys(2, 1), start(relay_z[1]), got_keys(2, 0)),
        5: lambda: got((2, rows, rows), 6),
        6: lambda: (got((3, 0, half), 7), got((3, half, half), 8), start(forward_far)),
        8: lambda: got((3, rows, rows), 9),
        12: lambda: (got_keys(3, 0), got_keys(3, 1)),
    }
    after = {
        8: lambda: stage_row(0),
        9: lambda: (start(kv_y[0]), stage_row(1)),
        10: lambda: start(kv_y[1]),
        11: lambda: stage_row(2),
        12: lambda: (start(kv_y[2]), sum_y(0), dq_core[3].start()),
        13: lambda: (sum_y(1), start(kv_z[0]), dq_core[2].start(), join_core(3)),
        14: lambda: (start(dq_x[3]), start(kv_z[1]), dq_core[1].start(), join_core(2)),
        15: lambda: (start(dq_x[2]), dq_core[0].start(), stage_row(3)),
    }

    def chosen(t, table):
        out = jnp.int32(table[1])
        for i in range(2, len(table)):
            out = jnp.where(t == i, table[i], out)
        return out

    def step(t, carry):
        p, r = chosen(t, PAIR), chosen(t, KEYS)
        for i, action in before.items():
            @pl.when(t == i)
            def _():
                action()

        near, far = (p + 1) // 2, (r + 1) // 2
        mid = near % 2
        q_blocks = [
            block((near, 4 - near)[j % 2], j // 2, 0, j % 2 * (1 - mid) + mid * (p - 1)) for j in range(4)
        ]
        k_blocks = [block(0, 0, (far, 4 - far)[h], b) for h in (0, 1) for b in (0, 1)]
        tile(r, p, 0, 2, q_blocks, k_blocks)

        for i, action in after.items():
            @pl.when(t == i)
            def _():
                action()

        return carry

    lax.fori_loop(1, 16, step, 0)

    sum_y(2)
    start(kv_y[3])
    start(kv_z[2])
    join_core(1)
    landed(core_in.at[0], core_sem.at[0])
    total = dq_acc[0, 0] + core_in[0]
    start(dq_x[1])
    for w in (0, 1):
        side = total[:, w * half : (w + 1) * half]
        for i in (1, 0, 2):
            landed(x_in.at[i, w], x_sem.at[i, w])
            side = side + x_in[i, w].astype(F32)
        dq_rows[w] = jnp.transpose(side * scale)
    dq_leave = pltpu.make_async_copy(dq_rows, dq_out.at[0], load_sem.at[0])
    sum_y(3)
    dq_leave.start()
    total = y_own[0, zhi]
    for i in (4, 1, 5, 3, 7):
        landed(z_in.at[i - 1], z_sem.at[i - 1])
        total = total + z_in[i - 1].astype(F32)
    start(kv_z[3])
    for i in (2, 6):
        landed(z_in.at[i - 1], z_sem.at[i - 1])
        total = total + z_in[i - 1].astype(F32)
    dkv_out[0] = total[:, :feat] * scale
    dkv_out[1] = total[:, feat:]
    dq_leave.wait()
    for copy in sends:
        copy.wait_send()


def finish(dq_in, dkv_in, dq_out, dk_out, dv_out, held, held_kv, in_sem, out_sem):
    half = held.shape[1]
    moves = [
        (dq_in.at[0, w], held.at[w], dq_out.at[0, pl.ds(w * half, half)]) for w in (0, 1)
    ] + [(dkv_in.at[i], held_kv.at[i], out) for i, out in enumerate((dk_out, dv_out))]
    arrivals = [
        pltpu.make_async_copy(src, at, in_sem.at[i]) for i, (src, at, _) in enumerate(moves)
    ]
    leaves = [
        pltpu.make_async_copy(at, dst, out_sem.at[i]) for i, (_, at, dst) in enumerate(moves)
    ]
    for copy in arrivals:
        copy.start()
    for arrival, leave in zip(arrivals, leaves):
        arrival.wait()
        leave.start()
    for leave in leaves:
        leave.wait()


def on_device(query, key, value, output, out_grad, lse, block_order):
    rows, feat = key.shape
    half, piece = rows // 2, rows // RING
    any_space = pl.BlockSpec(memory_space=pl.ANY)
    vmem = pl.BlockSpec(memory_space=pltpu.VMEM)
    dma = pltpu.SemaphoreType.DMA
    dq, dkv = pl.pallas_call(
        kernel,
        out_shape=(
            jax.ShapeDtypeStruct((1, 2, half, feat), F32),
            jax.ShapeDtypeStruct((2, piece, feat), F32),
        ),
        in_specs=[any_space] * 6 + [pl.BlockSpec(memory_space=pltpu.SMEM)],
        out_specs=(any_space, vmem),
        scratch_shapes=[
            pltpu.VMEM((4, 2 * rows, feat), BF16),
            pltpu.VMEM((4, 2 * rows, feat), BF16),
            pltpu.VMEM((4, 2, 2 * rows), F32),
            pltpu.VMEM((4, 2, Y, piece, feat), BF16),
            pltpu.VMEM((4, 2, Y, piece, feat), BF16),
            pltpu.VMEM((rows, feat), BF16),
            pltpu.VMEM((1, rows), F32),
            pltpu.VMEM((4, 2, feat, rows), F32),
            pltpu.VMEM((4, 2, Y, piece, feat), F32),
            pltpu.VMEM((4, 2, Y, piece, feat), F32),
            pltpu.VMEM((4, feat, rows), F32),
            pltpu.VMEM((3, 2, feat, half), BF16),
            pltpu.VMEM((3, 2, feat, half), BF16),
            pltpu.VMEM((4, Y, 2, piece, 2 * feat), BF16),
            pltpu.VMEM((4, 2, piece, 2 * feat), F32),
            pltpu.VMEM((4, Y - 1, 2, piece, 2 * feat), BF16),
            pltpu.VMEM((4, 2, piece, 2 * feat), BF16),
            pltpu.VMEM((RING - 1, piece, 2 * feat), BF16),
            pltpu.VMEM((2, half, feat), F32),
            dma((8,)),
            dma((80,)),
            dma((10,)),
            dma((10,)),
            dma((10,)),
            dma((4, 2)),
            dma((4, 2)),
            dma((4,)),
            dma((3, 2)),
            dma((4, Y - 1)),
            dma((RING - 1,)),
        ],
        compiler_params=pltpu.CompilerParams(
            collective_id=0, has_side_effects=True, vmem_limit_bytes=67043328
        ),
        name="attention_backward",
    )(
        query,
        key.reshape(Y, 2, piece, feat),
        value.reshape(Y, 2, piece, feat),
        output, out_grad, lse, block_order,
    )
    return pl.pallas_call(
        finish,
        out_shape=(
            jax.ShapeDtypeStruct((1, rows, feat), F32),
            jax.ShapeDtypeStruct((piece, feat), F32),
            jax.ShapeDtypeStruct((piece, feat), F32),
        ),
        in_specs=[any_space] * 2,
        out_specs=(any_space,) * 3,
        scratch_shapes=[
            pltpu.VMEM((2, half, feat), F32),
            pltpu.VMEM((2, piece, feat), F32),
            dma((4,)),
            dma((4,)),
        ],
        compiler_params=pltpu.CompilerParams(vmem_limit_bytes=67043328),
        name="finish",
    )(dq, dkv)


def solution(mesh):
    in_specs = (
        P("head", "blk", None),
        P("blk", None),
        P("blk", None),
        P("head", "blk", None),
        P("head", "blk", None),
        P("head", "blk"),
        P(),
    )
    out_specs = (P("head", "blk", None), P(("blk", "head"), None), P(("blk", "head"), None))
    return jax.shard_map(
        on_device, mesh=mesh, in_specs=in_specs, out_specs=out_specs, check_vma=False
    )
```

```python
import jax
import jax.numpy as jnp
from jax import lax
from jax.experimental import pallas as pl
from jax.experimental.pallas import tpu as pltpu
from jax.sharding import PartitionSpec as P

F32 = jnp.float32
BF16 = jnp.bfloat16
MESH = pl.DeviceIdType.MESH
LOG2E = 1.4426950408889634
DEAD = 1.0e9
PAIR = (0, 0, 1, 1, 0, 2, 2, 1, 3, 3, 2, 3, 3, 2, 1, 0)
KEYS = (0, 1, 0, 1, 2, 0, 1, 2, 0, 1, 2, 2, 3, 3, 3, 3)
X, Z, C, Y = 4, 4, 2, 4
RING = 8


def dot(left, right, left_dim, right_dim):
    return lax.dot_general(
        left, right, (((left_dim,), (right_dim,)), ((), ())), preferred_element_type=F32
    )


def kernel(
    q_hbm, k_hbm, v_hbm, o_hbm, g_hbm, l_hbm, order,
    dq_out, dkv_out,
    qb, gb, sb, kb, vb, ob, lb,
    dq_acc, dk_acc, dv_acc, core_in, x_out, x_in,
    y_out, y_own, y_in, z_out, z_in, dq_rows,
    load_sem, send_sem, q_sem, g_sem, s_sem, k_sem, v_sem, core_sem, x_sem, y_sem, z_sem, round_sem,
):
    rows, feat = ob.shape
    half, piece = rows // 2, rows // RING
    scale = feat ** -0.5
    blk = lax.axis_index("blk")
    head = lax.axis_index("head")
    core = blk % C
    zlo = (blk // C) % Z
    x = blk // (C * Z)
    zhi = head % 2
    y = head // 2
    ring = zhi * Z + zlo

    def at(dx=0, dc=0):
        return {"blk": (((x + dx) % X) * Z + zlo) * C + (core + dc) % C, "head": head}

    def at_y(dy):
        return {"blk": blk, "head": ((y + dy) % Y) * 2 + zhi}

    def at_ring(dz):
        there = (ring + dz) % RING
        return {"blk": (x * Z + there % Z) * C + core, "head": y * 2 + there // Z}

    beside = [at(dx=1), at(dx=3), at_y(1), at_y(3), at_ring(1), at_ring(7)]
    greeted = [at(dc=1)] + beside
    barrier = pltpu.get_barrier_semaphore()
    for device in greeted:
        pl.semaphore_signal(barrier, inc=1, device_id=device, device_id_type=MESH)

    loads = []
    own = pl.ds(0, rows)
    for src, dst in (
        (g_hbm.at[0], gb.at[0, own]), (o_hbm.at[0], ob), (l_hbm, lb), (q_hbm.at[0], qb.at[0, own]),
        (k_hbm.at[:, 0], kb.at[0, 0]), (v_hbm.at[:, 0], vb.at[0, 0]),
        (k_hbm.at[:, 1], kb.at[0, 1]), (v_hbm.at[:, 1], vb.at[0, 1]),
    ):
        loads.append(pltpu.make_async_copy(src, dst, load_sem.at[len(loads)]))
        loads[-1].start()

    sends = []

    def remote(src, dst, recv, device):
        copy = pltpu.make_async_remote_copy(
            src_ref=src, dst_ref=dst, send_sem=send_sem.at[len(sends)], recv_sem=recv,
            device_id=device, device_id_type=MESH,
        )
        sends.append(copy)
        return copy

    def landed(dst, recv):
        pltpu.make_async_remote_copy(
            src_ref=dst, dst_ref=dst, send_sem=send_sem.at[0], recv_sem=recv,
            device_id=at(dc=1), device_id_type=MESH,
        ).wait_recv()

    def send_round(i):
        for device in (beside, beside[4:], beside[4:])[i]:
            pl.semaphore_signal(round_sem.at[i], inc=1, device_id=device, device_id_type=MESH)

    def wait_round(i):
        pl.semaphore_wait(round_sem.at[i], (6, 2, 2)[i])

    def start(copies):
        for copy in copies:
            copy.start()

    def part(buf, place):
        p, first, count = place
        return buf.at[p, pl.ds(first, count)]

    def stat(place):
        p, first, count = place
        return sb.at[p, :, pl.ds(first, count)]

    def pass_q(src, dst, i, device):
        return remote(part(qb, src), part(qb, dst), q_sem.at[i], device)

    def pass_g(src, dst, i, device):
        return remote(part(gb, src), part(gb, dst), g_sem.at[i], device)

    def pass_s(src, dst, i, device):
        return remote(stat(src), stat(dst), s_sem.at[i], device)

    def pass_all(src, dst, i, device):
        return [f(src, dst, i, device) for f in (pass_q, pass_g, pass_s)]

    def got(place, i):
        landed(part(qb, place), q_sem.at[i])
        landed(part(gb, place), g_sem.at[i])
        landed(stat(place), s_sem.at[i])

    def got_keys(r, h):
        landed(kb.at[r, h], k_sem.at[r, h])
        landed(vb.at[r, h], v_sem.at[r, h])

    to_core = pass_all((0, 0, rows), (0, rows, rows), 0, at(dc=1))
    waves, keys_out, forward, relay_x, relay_z = [], [], [], [], []
    for w in (0, 1):
        mine, p, i = (0, w * half, half), 1 + w, 3 * w + 1
        right = pass_all(mine, (p, half, half), i + 1, at(dx=1))
        left = pass_all(mine, (p, 0, half), i, at(dx=3))
        waves.append((right, left))
        keys_out.append([
            remote(buf.at[0, w], buf.at[p, h], sem.at[p, h], at_ring(dz))
            for buf, sem in ((kb, k_sem), (vb, v_sem)) for h, dz in ((1, 1), (0, 7))
        ])
        forward.append(pass_all((p, 0, rows), (p, rows, rows), i + 2, at(dc=1)))
        far = (3, w * half, half)
        relay_x.append([
            pass_q((p, 0, half), far, 7 + w, at(dx=3)),
            pass_g((p, half, half), far, 7 + w, at(dx=1)),
            pass_s((p, 0, half), far, 7 + w, at(dx=3)),
        ])
        relay_z.append([
            remote(buf.at[p, w], buf.at[3, w], sem.at[3, w], at_ring((7, 1)[w]))
            for buf, sem in ((kb, k_sem), (vb, v_sem))
        ])
    forward_far = pass_all((3, 0, rows), (3, rows, rows), 9, at(dc=1))
    dq_core = [remote(dq_acc.at[p, 1], core_in.at[p], core_sem.at[p], at(dc=1)) for p in range(4)]
    dq_x = [None] + [
        [remote(x_out.at[w, i], x_in.at[2 * i, w], x_sem.at[2 * i, w], at(dx=(1, 3)[i])) for i in (0, 1)]
        for w in (0, 1)
    ] + [[remote(x_out.at[2, w], x_in.at[1, w], x_sem.at[1, w], at(dx=2)) for w in (0, 1)]]
    kv_y = [
        [remote(y_out.at[r, (y + i) % Y], y_in.at[r, i - 1], y_sem.at[r, i - 1], at_y(i)) for i in (2, 1, 3)]
        for r in range(4)
    ]
    kv_z = [[remote(z_out.at[0, 1 - zhi], z_in.at[Z - 1], z_sem.at[Z - 1], at_ring(Z))]]
    for r, targets in ((1, ((1, 0), (3, 0))), (2, ((1, 1), (3, 1))), (3, ((2, 0), (2, 1)))):
        kv_z.append([])
        for h, (dz, side) in enumerate(targets):
            ahead = (side * Z + (zlo + dz) % Z - ring + RING) % RING
            kv_z[r].append(
                remote(z_out.at[r, h], z_in.at[ahead - 1], z_sem.at[ahead - 1], at_ring(ahead))
            )

    for i in (0, 1, 2):
        loads[i].wait()
    delta = jnp.sum(jnp.transpose(gb[0, own].astype(F32) * ob[...].astype(F32)), axis=0, keepdims=True)
    sb[0, 0:1, own] = lb[...] * LOG2E
    sb[0, 1:2, own] = delta
    for i in range(3, 8):
        loads[i].wait()
    pl.semaphore_wait(barrier, len(greeted))

    start(to_core[:2])
    for w in (0, 1):
        right, left = waves[w]
        start([right[0], left[0], right[1], left[1]])
        start(keys_out[w])
        if w == 0:
            dq_acc[...] = jnp.zeros_like(dq_acc)
            start([to_core[2]])
        start([right[2], left[2]])
    send_round(0)
    dk_acc[...] = jnp.zeros_like(dk_acc)
    dv_acc[...] = jnp.zeros_like(dv_acc)

    def block(dx, dc, dz, b):
        return order[2 * (((x + dx) % X * Z + (zlo + dz) % Z) * C + (core + dc) % C) + b]

    def grads(r, keys, vals, q_rows, g_rows, probs, d_row):
        dprobs = dot(vals, g_rows, 1, 1)
        dscores = (probs * (dprobs - d_row)).astype(BF16)
        dv_acc[r] += dot(probs.astype(BF16), g_rows, 1, 0).reshape(2, Y, piece, feat)
        dk_acc[r] += dot(dscores, q_rows, 1, 0).reshape(2, Y, piece, feat)
        return dot(keys, dscores, 0, 0)

    def biased(l_row, q_blocks, k_block):
        parts = []
        for i, q_block in enumerate(q_blocks):
            dead = jnp.where(q_block > k_block, 0.0, DEAD)
            parts.append(l_row[:, i * half : (i + 1) * half] + dead)
        return jnp.concatenate(parts, axis=1)

    def tile(r, p, first, count, q_blocks, k_blocks):
        cols = pl.ds(first * rows, count * rows)
        keys, vals = kb[r].reshape(rows, feat), vb[r].reshape(rows, feat)
        q_rows, g_rows = qb[p, cols], gb[p, cols]
        l_row, d_row = sb[p, 0:1, cols], sb[p, 1:2, cols]
        lows = jnp.stack([biased(l_row, q_blocks, b) for b in k_blocks])
        scores = dot(keys, q_rows, 1, 1).reshape(4, half // 2, count * rows)
        probs = jnp.exp2(scores * (scale * LOG2E) - lows).reshape(rows, count * rows)
        part_q = grads(r, keys, vals, q_rows, g_rows, probs, d_row)
        for i in range(count):
            dq_acc[p, first + i] += part_q[:, i * rows : (i + 1) * rows]

    own_blocks = [block(0, 0, 0, b) for b in (0, 1)]
    q_rows, g_rows = qb[0, own], gb[0, own]
    at_row = lax.broadcasted_iota(jnp.int32, (rows, 1), 0)
    at_col = lax.broadcasted_iota(jnp.int32, (1, rows), 1)
    quarter = at_row % half // piece
    k_off = quarter % 2 * (2 * piece) + at_row // half * piece + at_row % piece
    k_pos = jnp.where(quarter < 2, own_blocks[0], own_blocks[1]) * half + k_off
    q_pos = jnp.where(at_col < half, own_blocks[0], own_blocks[1]) * half + at_col % half
    keys, vals = kb[0].reshape(rows, feat), vb[0].reshape(rows, feat)
    scores = dot(keys, q_rows, 1, 1)
    probs = jnp.where(
        q_pos >= k_pos, jnp.exp2(scores * (scale * LOG2E) - sb[0, 0:1, own]), 0.0
    )
    dq_acc[0, 0] += grads(0, keys, vals, q_rows, g_rows, probs, sb[0, 1:2, own])

    got((0, rows, rows), 0)
    tile(0, 0, 1, 1, [block(0, 1, 0, b) for b in (0, 1)], own_blocks * 2)

    def stage_row(r):
        for h in (0, 1):
            y_out[r, :, h, :, :feat] = dk_acc[r, h].astype(BF16)
            y_out[r, :, h, :, feat:] = dv_acc[r, h].astype(BF16)
            y_own[r, h, :, :feat] = dk_acc[r, h, y]
            y_own[r, h, :, feat:] = dv_acc[r, h, y]

    def sum_y(r):
        total = y_own[r]
        for i in range(Y - 1):
            landed(y_in.at[r, i], y_sem.at[r, i])
            total = total + y_in[r, i].astype(F32)
        z_out[r] = total.astype(BF16)
        if r == 0:
            y_own[0] = total

    def join_core(p):
        landed(core_in.at[p], core_sem.at[p])
        total = (dq_acc[p, 0] + core_in[p]).astype(BF16)
        x_out[p - 1, 0] = total[:, :half]
        x_out[p - 1, 1] = total[:, half:]

    before = {
        1: lambda: (
            got((1, 0, half), 1), got((1, half, half), 2), start(forward[0]), start(relay_x[0]),
            got_keys(1, 0), start(relay_z[0]), got_keys(1, 1),
        ),
        2: lambda: got((1, rows, rows), 3),
        3: lambda: (
            got((2, 0, half), 4), got((2, half, half), 5), start(forward[1]), start(relay_x[1]),
        ),
        4: lambda: (wait_round(0), send_round(1), got_keys(2, 1), start(relay_z[1]), got_keys(2, 0)),
        5: lambda: (wait_round(1), send_round(2), got((2, rows, rows), 6)),
        6: lambda: (wait_round(2), got((3, 0, half), 7), got((3, half, half), 8), start(forward_far)),
        8: lambda: got((3, rows, rows), 9),
        12: lambda: (got_keys(3, 0), got_keys(3, 1)),
    }
    after = {
        8: lambda: stage_row(0),
        9: lambda: (start(kv_y[0]), stage_row(1)),
        10: lambda: start(kv_y[1]),
        11: lambda: stage_row(2),
        12: lambda: (start(kv_y[2]), dq_core[3].start()),
        13: lambda: dq_core[2].start(),
        14: lambda: (dq_core[1].start(), join_core(3), sum_y(0), start(dq_x[3])),
        15: lambda: (dq_core[0].start(), join_core(2), stage_row(3)),
    }

    def chosen(t, table):
        out = jnp.int32(table[1])
        for i in range(2, len(table)):
            out = jnp.where(t == i, table[i], out)
        return out

    def step(t, carry):
        p, r = chosen(t, PAIR), chosen(t, KEYS)
        for i, action in before.items():
            @pl.when(t == i)
            def _():
                action()

        near, far = (p + 1) // 2, (r + 1) // 2
        mid = near % 2
        q_blocks = [
            block((near, 4 - near)[j % 2], j // 2, 0, j % 2 * (1 - mid) + mid * (p - 1)) for j in range(4)
        ]
        k_blocks = [block(0, 0, (far, 4 - far)[h], b) for h in (0, 1) for b in (0, 1)]
        tile(r, p, 0, 2, q_blocks, k_blocks)

        for i, action in after.items():
            @pl.when(t == i)
            def _():
                action()

        return carry

    lax.fori_loop(1, 16, step, 0)

    sum_y(1)
    start(kv_y[3])
    start(dq_x[2])
    start(kv_z[0])
    start(kv_z[1])
    join_core(1)
    sum_y(2)
    start(dq_x[1])
    start(kv_z[2])
    landed(core_in.at[0], core_sem.at[0])
    total = dq_acc[0, 0] + core_in[0]
    for w in (0, 1):
        side = total[:, w * half : (w + 1) * half]
        for i in (1, 0, 2):
            landed(x_in.at[i, w], x_sem.at[i, w])
            side = side + x_in[i, w].astype(F32)
        dq_rows[w] = jnp.transpose(side * scale)
    dq_leave = pltpu.make_async_copy(dq_rows, dq_out.at[0], load_sem.at[0])
    sum_y(3)
    dq_leave.start()
    total = y_own[0, zhi]
    for i in (4, 1, 5, 3, 7):
        landed(z_in.at[i - 1], z_sem.at[i - 1])
        total = total + z_in[i - 1].astype(F32)
    start(kv_z[3])
    for i in (2, 6):
        landed(z_in.at[i - 1], z_sem.at[i - 1])
        total = total + z_in[i - 1].astype(F32)
    dkv_out[0] = total[:, :feat] * scale
    dkv_out[1] = total[:, feat:]
    dq_leave.wait()
    for copy in sends:
        copy.wait_send()


def finish(dq_in, dkv_in, dq_out, dk_out, dv_out, held, held_kv, in_sem, out_sem):
    half = held.shape[1]
    moves = [
        (dq_in.at[0, w], held.at[w], dq_out.at[0, pl.ds(w * half, half)]) for w in (0, 1)
    ] + [(dkv_in.at[i], held_kv.at[i], out) for i, out in enumerate((dk_out, dv_out))]
    arrivals = [
        pltpu.make_async_copy(src, at, in_sem.at[i]) for i, (src, at, _) in enumerate(moves)
    ]
    leaves = [
        pltpu.make_async_copy(at, dst, out_sem.at[i]) for i, (_, at, dst) in enumerate(moves)
    ]
    for copy in arrivals:
        copy.start()
    for arrival, leave in zip(arrivals, leaves):
        arrival.wait()
        leave.start()
    for leave in leaves:
        leave.wait()


def on_device(query, key, value, output, out_grad, lse, block_order):
    rows, feat = key.shape
    half, piece = rows // 2, rows // RING
    any_space = pl.BlockSpec(memory_space=pl.ANY)
    vmem = pl.BlockSpec(memory_space=pltpu.VMEM)
    dma = pltpu.SemaphoreType.DMA
    dq, dkv = pl.pallas_call(
        kernel,
        out_shape=(
            jax.ShapeDtypeStruct((1, 2, half, feat), F32),
            jax.ShapeDtypeStruct((2, piece, feat), F32),
        ),
        in_specs=[any_space] * 6 + [pl.BlockSpec(memory_space=pltpu.SMEM)],
        out_specs=(any_space, vmem),
        scratch_shapes=[
            pltpu.VMEM((4, 2 * rows, feat), BF16),
            pltpu.VMEM((4, 2 * rows, feat), BF16),
            pltpu.VMEM((4, 2, 2 * rows), F32),
            pltpu.VMEM((4, 2, Y, piece, feat), BF16),
            pltpu.VMEM((4, 2, Y, piece, feat), BF16),
            pltpu.VMEM((rows, feat), BF16),
            pltpu.VMEM((1, rows), F32),
            pltpu.VMEM((4, 2, feat, rows), F32),
            pltpu.VMEM((4, 2, Y, piece, feat), F32),
            pltpu.VMEM((4, 2, Y, piece, feat), F32),
            pltpu.VMEM((4, feat, rows), F32),
            pltpu.VMEM((3, 2, feat, half), BF16),
            pltpu.VMEM((3, 2, feat, half), BF16),
            pltpu.VMEM((4, Y, 2, piece, 2 * feat), BF16),
            pltpu.VMEM((4, 2, piece, 2 * feat), F32),
            pltpu.VMEM((4, Y - 1, 2, piece, 2 * feat), BF16),
            pltpu.VMEM((4, 2, piece, 2 * feat), BF16),
            pltpu.VMEM((RING - 1, piece, 2 * feat), BF16),
            pltpu.VMEM((2, half, feat), F32),
            dma((8,)),
            dma((80,)),
            dma((10,)),
            dma((10,)),
            dma((10,)),
            dma((4, 2)),
            dma((4, 2)),
            dma((4,)),
            dma((3, 2)),
            dma((4, Y - 1)),
            dma((RING - 1,)),
            pltpu.SemaphoreType.REGULAR((3,)),
        ],
        compiler_params=pltpu.CompilerParams(
            collective_id=0, has_side_effects=True, vmem_limit_bytes=67043328
        ),
        name="attention_backward",
    )(
        query,
        key.reshape(Y, 2, piece, feat),
        value.reshape(Y, 2, piece, feat),
        output, out_grad, lse, block_order,
    )
    return pl.pallas_call(
        finish,
        out_shape=(
            jax.ShapeDtypeStruct((1, rows, feat), F32),
            jax.ShapeDtypeStruct((piece, feat), F32),
            jax.ShapeDtypeStruct((piece, feat), F32),
        ),
        in_specs=[any_space] * 2,
        out_specs=(any_space,) * 3,
        scratch_shapes=[
            pltpu.VMEM((2, half, feat), F32),
            pltpu.VMEM((2, piece, feat), F32),
            dma((4,)),
            dma((4,)),
        ],
        compiler_params=pltpu.CompilerParams(vmem_limit_bytes=67043328),
        name="finish",
    )(dq, dkv)


def solution(mesh):
    in_specs = (
        P("head", "blk", None),
        P("blk", None),
        P("blk", None),
        P("head", "blk", None),
        P("head", "blk", None),
        P("head", "blk"),
        P(),
    )
    out_specs = (P("head", "blk", None), P(("blk", "head"), None), P(("blk", "head"), None))
    return jax.shard_map(
        on_device, mesh=mesh, in_specs=in_specs, out_specs=out_specs, check_vma=False
    )
```

```python
import jax
import jax.numpy as jnp
from jax import lax
from jax.experimental import pallas as pl
from jax.experimental.pallas import tpu as pltpu
from jax.sharding import PartitionSpec as P

F32 = jnp.float32
BF16 = jnp.bfloat16
MESH = pl.DeviceIdType.MESH
LOG2E = 1.4426950408889634
DEAD = 1.0e9
PAIR = (0, 0, 1, 1, 0, 2, 2, 1, 3, 3, 2, 3, 3, 2)
KEYS = (0, 1, 0, 1, 2, 0, 1, 2, 0, 1, 2, 2, 3, 3)
X, Z, C, Y = 4, 4, 2, 4
RING = 8


def dot(left, right, left_dim, right_dim):
    return lax.dot_general(
        left, right, (((left_dim,), (right_dim,)), ((), ())), preferred_element_type=F32
    )


def kernel(
    q_hbm, k_hbm, v_hbm, o_hbm, g_hbm, l_hbm, order,
    dq_out, dkv_out,
    qb, gb, sb, kb, vb, ob, lb,
    dq_acc, dk_acc, dv_acc, core_in, x_out, x_in,
    y_out, y_own, y_in, z_out, z_in, dq_rows,
    load_sem, send_sem, q_sem, g_sem, s_sem, k_sem, v_sem, core_sem, x_sem, y_sem, z_sem, round_sem,
):
    rows, feat = ob.shape
    half, piece = rows // 2, rows // RING
    scale = feat ** -0.5
    blk = lax.axis_index("blk")
    head = lax.axis_index("head")
    core = blk % C
    zlo = (blk // C) % Z
    x = blk // (C * Z)
    zhi = head % 2
    y = head // 2
    ring = zhi * Z + zlo

    def at(dx=0, dc=0):
        return {"blk": (((x + dx) % X) * Z + zlo) * C + (core + dc) % C, "head": head}

    def at_y(dy):
        return {"blk": blk, "head": ((y + dy) % Y) * 2 + zhi}

    def at_ring(dz):
        there = (ring + dz) % RING
        return {"blk": (x * Z + there % Z) * C + core, "head": y * 2 + there // Z}

    beside = [at(dx=1), at(dx=3), at_y(1), at_y(3), at_ring(1), at_ring(7)]
    greeted = [at(dc=1)] + beside
    barrier = pltpu.get_barrier_semaphore()
    for device in greeted:
        pl.semaphore_signal(barrier, inc=1, device_id=device, device_id_type=MESH)

    loads = []
    own = pl.ds(0, rows)
    for src, dst in (
        (g_hbm.at[0], gb.at[0, own]), (o_hbm.at[0], ob), (l_hbm, lb), (q_hbm.at[0], qb.at[0, own]),
        (k_hbm.at[:, 0], kb.at[0, 0]), (v_hbm.at[:, 0], vb.at[0, 0]),
        (k_hbm.at[:, 1], kb.at[0, 1]), (v_hbm.at[:, 1], vb.at[0, 1]),
    ):
        loads.append(pltpu.make_async_copy(src, dst, load_sem.at[len(loads)]))
        loads[-1].start()

    sends = []

    def remote(src, dst, recv, device):
        copy = pltpu.make_async_remote_copy(
            src_ref=src, dst_ref=dst, send_sem=send_sem.at[len(sends)], recv_sem=recv,
            device_id=device, device_id_type=MESH,
        )
        sends.append(copy)
        return copy

    def landed(dst, recv):
        pltpu.make_async_remote_copy(
            src_ref=dst, dst_ref=dst, send_sem=send_sem.at[0], recv_sem=recv,
            device_id=at(dc=1), device_id_type=MESH,
        ).wait_recv()

    def send_round(i):
        for device in (beside, beside[4:], beside[4:])[i]:
            pl.semaphore_signal(round_sem.at[i], inc=1, device_id=device, device_id_type=MESH)

    def wait_round(i):
        pl.semaphore_wait(round_sem.at[i], (6, 2, 2)[i])

    def start(copies):
        for copy in copies:
            copy.start()

    def part(buf, place):
        p, first, count = place
        return buf.at[p, pl.ds(first, count)]

    def stat(place):
        p, first, count = place
        return sb.at[p, :, pl.ds(first, count)]

    def pass_q(src, dst, i, device):
        return remote(part(qb, src), part(qb, dst), q_sem.at[i], device)

    def pass_g(src, dst, i, device):
        return remote(part(gb, src), part(gb, dst), g_sem.at[i], device)

    def pass_s(src, dst, i, device):
        return remote(stat(src), stat(dst), s_sem.at[i], device)

    def pass_all(src, dst, i, device):
        return [f(src, dst, i, device) for f in (pass_q, pass_g, pass_s)]

    def got(place, i):
        landed(part(qb, place), q_sem.at[i])
        landed(part(gb, place), g_sem.at[i])
        landed(stat(place), s_sem.at[i])

    def got_keys(r, h):
        landed(kb.at[r, h], k_sem.at[r, h])
        landed(vb.at[r, h], v_sem.at[r, h])

    to_core = pass_all((0, 0, rows), (0, rows, rows), 0, at(dc=1))
    waves, keys_out, forward, relay_x, relay_z = [], [], [], [], []
    for w in (0, 1):
        mine, p, i = (0, w * half, half), 1 + w, 3 * w + 1
        right = pass_all(mine, (p, half, half), i + 1, at(dx=1))
        left = pass_all(mine, (p, 0, half), i, at(dx=3))
        waves.append((right, left))
        keys_out.append([
            remote(buf.at[0, w], buf.at[p, h], sem.at[p, h], at_ring(dz))
            for buf, sem in ((kb, k_sem), (vb, v_sem)) for h, dz in ((1, 1), (0, 7))
        ])
        forward.append(pass_all((p, 0, rows), (p, rows, rows), i + 2, at(dc=1)))
        far = (3, w * half, half)
        relay_x.append([
            pass_q((p, 0, half), far, 7 + w, at(dx=3)),
            pass_g((p, half, half), far, 7 + w, at(dx=1)),
            pass_s((p, 0, half), far, 7 + w, at(dx=3)),
        ])
        relay_z.append([
            remote(buf.at[p, w], buf.at[3, w], sem.at[3, w], at_ring((7, 1)[w]))
            for buf, sem in ((kb, k_sem), (vb, v_sem))
        ])
    forward_far = pass_all((3, 0, rows), (3, rows, rows), 9, at(dc=1))
    dq_core = [remote(dq_acc.at[p, 1], core_in.at[p], core_sem.at[p], at(dc=1)) for p in range(4)]
    dq_x = [None] + [
        [remote(x_out.at[w, i], x_in.at[2 * i, w], x_sem.at[2 * i, w], at(dx=(1, 3)[i])) for i in (0, 1)]
        for w in (0, 1)
    ] + [[remote(x_out.at[2, w], x_in.at[1, w], x_sem.at[1, w], at(dx=2)) for w in (0, 1)]]
    kv_y = [
        [remote(y_out.at[r, (y + i) % Y], y_in.at[r, i - 1], y_sem.at[r, i - 1], at_y(i)) for i in (2, 1, 3)]
        for r in range(3)
    ]
    kv_y_last = [
        [
            remote(
                y_out.at[3, (y + i) % Y, h], y_in.at[3, i - 1, h], y_sem.at[3 + h, i - 1], at_y(i)
            )
            for i in (2, 1, 3)
        ]
        for h in (0, 1)
    ]
    kv_z = [[remote(z_out.at[0, 1 - zhi], z_in.at[Z - 1], z_sem.at[Z - 1], at_ring(Z))]]
    for r, targets in ((1, ((1, 0), (3, 0))), (2, ((1, 1), (3, 1))), (3, ((2, 0), (2, 1)))):
        kv_z.append([])
        for h, (dz, side) in enumerate(targets):
            ahead = (side * Z + (zlo + dz) % Z - ring + RING) % RING
            kv_z[r].append(
                remote(z_out.at[r, h], z_in.at[ahead - 1], z_sem.at[ahead - 1], at_ring(ahead))
            )

    for i in (0, 1, 2):
        loads[i].wait()
    delta = jnp.sum(jnp.transpose(gb[0, own].astype(F32) * ob[...].astype(F32)), axis=0, keepdims=True)
    sb[0, 0:1, own] = lb[...] * LOG2E
    sb[0, 1:2, own] = delta
    for i in range(3, 8):
        loads[i].wait()
    pl.semaphore_wait(barrier, len(greeted))

    start(to_core[:2])
    for w in (0, 1):
        right, left = waves[w]
        start([right[0], left[0], right[1], left[1]])
        start(keys_out[w])
        if w == 0:
            dq_acc[...] = jnp.zeros_like(dq_acc)
            start([to_core[2]])
        start([right[2], left[2]])
    send_round(0)
    dk_acc[...] = jnp.zeros_like(dk_acc)
    dv_acc[...] = jnp.zeros_like(dv_acc)

    def block(dx, dc, dz, b):
        return order[2 * (((x + dx) % X * Z + (zlo + dz) % Z) * C + (core + dc) % C) + b]

    def grads(kv_at, keys, vals, q_rows, g_rows, probs, d_row):
        dprobs = dot(vals, g_rows, 1, 1)
        dscores = (probs * (dprobs - d_row)).astype(BF16)
        shape = dv_acc.at[kv_at].shape
        dv_acc[kv_at] += dot(probs.astype(BF16), g_rows, 1, 0).reshape(shape)
        dk_acc[kv_at] += dot(dscores, q_rows, 1, 0).reshape(shape)
        return dot(keys, dscores, 0, 0)

    def biased(l_row, q_blocks, k_block):
        parts = []
        for i, q_block in enumerate(q_blocks):
            dead = jnp.where(q_block > k_block, 0.0, DEAD)
            parts.append(l_row[:, i * half : (i + 1) * half] + dead)
        return jnp.concatenate(parts, axis=1)

    def tile(kv_at, p, first, count, q_blocks, k_blocks):
        cols = pl.ds(first * rows, count * rows)
        keys, vals = kb[kv_at].reshape(-1, feat), vb[kv_at].reshape(-1, feat)
        q_rows, g_rows = qb[p, cols], gb[p, cols]
        l_row, d_row = sb[p, 0:1, cols], sb[p, 1:2, cols]
        lows = jnp.stack([biased(l_row, q_blocks, b) for b in k_blocks])
        scores = dot(keys, q_rows, 1, 1).reshape(len(k_blocks), half // 2, count * rows)
        probs = jnp.exp2(scores * (scale * LOG2E) - lows).reshape(-1, count * rows)
        part_q = grads(kv_at, keys, vals, q_rows, g_rows, probs, d_row)
        for i in range(count):
            dq_acc[p, first + i] += part_q[:, i * rows : (i + 1) * rows]

    own_blocks = [block(0, 0, 0, b) for b in (0, 1)]
    q_rows, g_rows = qb[0, own], gb[0, own]
    at_row = lax.broadcasted_iota(jnp.int32, (rows, 1), 0)
    at_col = lax.broadcasted_iota(jnp.int32, (1, rows), 1)
    quarter = at_row % half // piece
    k_off = quarter % 2 * (2 * piece) + at_row // half * piece + at_row % piece
    k_pos = jnp.where(quarter < 2, own_blocks[0], own_blocks[1]) * half + k_off
    q_pos = jnp.where(at_col < half, own_blocks[0], own_blocks[1]) * half + at_col % half
    keys, vals = kb[0].reshape(rows, feat), vb[0].reshape(rows, feat)
    scores = dot(keys, q_rows, 1, 1)
    probs = jnp.where(
        q_pos >= k_pos, jnp.exp2(scores * (scale * LOG2E) - sb[0, 0:1, own]), 0.0
    )
    dq_acc[0, 0] += grads((0,), keys, vals, q_rows, g_rows, probs, sb[0, 1:2, own])

    got((0, rows, rows), 0)
    tile((0,), 0, 1, 1, [block(0, 1, 0, b) for b in (0, 1)], own_blocks * 2)

    def stage(r, h):
        y_out[r, :, h, :, :feat] = dk_acc[r, h].astype(BF16)
        y_out[r, :, h, :, feat:] = dv_acc[r, h].astype(BF16)
        y_own[r, h, :, :feat] = dk_acc[r, h, y]
        y_own[r, h, :, feat:] = dv_acc[r, h, y]

    def stage_row(r):
        stage(r, 0)
        stage(r, 1)

    def sum_y(r):
        total = y_own[r]
        for i in range(Y - 1):
            landed(y_in.at[r, i], y_sem.at[r, i])
            total = total + y_in[r, i].astype(F32)
        z_out[r] = total.astype(BF16)
        if r == 0:
            y_own[0] = total

    def sum_y_last(h):
        total = y_own[3, h]
        for i in range(Y - 1):
            landed(y_in.at[3, i, h], y_sem.at[3 + h, i])
            total = total + y_in[3, i, h].astype(F32)
        z_out[3, h] = total.astype(BF16)

    def join_core(p):
        landed(core_in.at[p], core_sem.at[p])
        total = (dq_acc[p, 0] + core_in[p]).astype(BF16)
        x_out[p - 1, 0] = total[:, :half]
        x_out[p - 1, 1] = total[:, half:]

    before = {
        1: lambda: (
            got((1, 0, half), 1), got((1, half, half), 2), start(forward[0]), start(relay_x[0]),
            got_keys(1, 0), start(relay_z[0]), got_keys(1, 1),
        ),
        2: lambda: got((1, rows, rows), 3),
        3: lambda: (
            got((2, 0, half), 4), got((2, half, half), 5), start(forward[1]), start(relay_x[1]),
        ),
        4: lambda: (wait_round(0), send_round(1), got_keys(2, 1), start(relay_z[1]), got_keys(2, 0)),
        5: lambda: (wait_round(1), send_round(2), got((2, rows, rows), 6)),
        6: lambda: (wait_round(2), got((3, 0, half), 7), got((3, half, half), 8), start(forward_far)),
        8: lambda: got((3, rows, rows), 9),
        12: lambda: (got_keys(3, 0), got_keys(3, 1)),
    }
    after = {
        8: lambda: stage_row(0),
        9: lambda: (start(kv_y[0]), stage_row(1)),
        10: lambda: start(kv_y[1]),
        11: lambda: stage_row(2),
        12: lambda: (start(kv_y[2]), dq_core[3].start()),
        13: lambda: (dq_core[2].start(), sum_y(0)),
    }
    after_half = {
        0: lambda: (start(kv_z[0]), join_core(3)),
        1: lambda: (start(dq_x[3]), stage(3, 0)),
        2: lambda: (dq_core[1].start(), start(kv_y_last[0]), join_core(2)),
        3: lambda: (start(dq_x[2]), dq_core[0].start(), stage(3, 1)),
    }

    def chosen(t, table):
        out = jnp.int32(table[1])
        for i in range(2, len(table)):
            out = jnp.where(t == i, table[i], out)
        return out

    def pair_blocks(p):
        near = (p + 1) // 2
        mid = near % 2
        return [
            block((near, 4 - near)[j % 2], j // 2, 0, j % 2 * (1 - mid) + mid * (p - 1)) for j in range(4)
        ]

    def step(t, carry):
        p, r = chosen(t, PAIR), chosen(t, KEYS)
        for i, action in before.items():
            @pl.when(t == i)
            def _():
                action()

        far = (r + 1) // 2
        k_blocks = [block(0, 0, (far, 4 - far)[h], b) for h in (0, 1) for b in (0, 1)]
        tile((r,), p, 0, 2, pair_blocks(p), k_blocks)

        for i, action in after.items():
            @pl.when(t == i)
            def _():
                action()

        return carry

    lax.fori_loop(1, len(PAIR), step, 0)

    def half_step(t, carry):
        p, h = 1 - t % 2, t // 2
        tile((3, h), p, 0, 2, pair_blocks(p), [block(0, 0, 2, b) for b in (0, 1)])
        for i, action in after_half.items():
            @pl.when(t == i)
            def _():
                action()

        return carry

    lax.fori_loop(0, 4, half_step, 0)

    sum_y(1)
    start(kv_y_last[1])
    start(kv_z[1])
    join_core(1)
    sum_y(2)
    start(dq_x[1])
    start(kv_z[2])
    sum_y_last(0)
    landed(core_in.at[0], core_sem.at[0])
    dq_acc[0, 0, :, :half] += core_in[0, :, :half]
    start(kv_z[3][:1])
    sum_y_last(1)
    dq_acc[0, 0, :, half:] += core_in[0, :, half:]
    start(kv_z[3][1:])
    for w in (0, 1):
        side = dq_acc[0, 0, :, w * half : (w + 1) * half]
        for i in (1, 0, 2):
            landed(x_in.at[i, w], x_sem.at[i, w])
            side = side + x_in[i, w].astype(F32)
        dq_rows[w] = jnp.transpose(side * scale)
    total = y_own[0, zhi]
    for i in (4, 1, 5, 3, 7):
        landed(z_in.at[i - 1], z_sem.at[i - 1])
        total = total + z_in[i - 1].astype(F32)
    dq_leave = pltpu.make_async_copy(dq_rows, dq_out.at[0], load_sem.at[0])
    dq_leave.start()
    for i in (2, 6):
        landed(z_in.at[i - 1], z_sem.at[i - 1])
        total = total + z_in[i - 1].astype(F32)
    dkv_out[0] = total[:, :feat] * scale
    dkv_out[1] = total[:, feat:]
    dq_leave.wait()
    for copy in sends:
        copy.wait_send()


def finish(dq_in, dkv_in, dq_out, dk_out, dv_out, held, held_kv, in_sem, out_sem):
    half = held.shape[1]
    moves = [
        (dq_in.at[0, w], held.at[w], dq_out.at[0, pl.ds(w * half, half)]) for w in (0, 1)
    ] + [(dkv_in.at[i], held_kv.at[i], out) for i, out in enumerate((dk_out, dv_out))]
    arrivals = [
        pltpu.make_async_copy(src, at, in_sem.at[i]) for i, (src, at, _) in enumerate(moves)
    ]
    leaves = [
        pltpu.make_async_copy(at, dst, out_sem.at[i]) for i, (_, at, dst) in enumerate(moves)
    ]
    for copy in arrivals:
        copy.start()
    for arrival, leave in zip(arrivals, leaves):
        arrival.wait()
        leave.start()
    for leave in leaves:
        leave.wait()


def on_device(query, key, value, output, out_grad, lse, block_order):
    rows, feat = key.shape
    half, piece = rows // 2, rows // RING
    any_space = pl.BlockSpec(memory_space=pl.ANY)
    vmem = pl.BlockSpec(memory_space=pltpu.VMEM)
    dma = pltpu.SemaphoreType.DMA
    dq, dkv = pl.pallas_call(
        kernel,
        out_shape=(
            jax.ShapeDtypeStruct((1, 2, half, feat), F32),
            jax.ShapeDtypeStruct((2, piece, feat), F32),
        ),
        in_specs=[any_space] * 6 + [pl.BlockSpec(memory_space=pltpu.SMEM)],
        out_specs=(any_space, vmem),
        scratch_shapes=[
            pltpu.VMEM((4, 2 * rows, feat), BF16),
            pltpu.VMEM((4, 2 * rows, feat), BF16),
            pltpu.VMEM((4, 2, 2 * rows), F32),
            pltpu.VMEM((4, 2, Y, piece, feat), BF16),
            pltpu.VMEM((4, 2, Y, piece, feat), BF16),
            pltpu.VMEM((rows, feat), BF16),
            pltpu.VMEM((1, rows), F32),
            pltpu.VMEM((4, 2, feat, rows), F32),
            pltpu.VMEM((4, 2, Y, piece, feat), F32),
            pltpu.VMEM((4, 2, Y, piece, feat), F32),
            pltpu.VMEM((4, feat, rows), F32),
            pltpu.VMEM((3, 2, feat, half), BF16),
            pltpu.VMEM((3, 2, feat, half), BF16),
            pltpu.VMEM((4, Y, 2, piece, 2 * feat), BF16),
            pltpu.VMEM((4, 2, piece, 2 * feat), F32),
            pltpu.VMEM((4, Y - 1, 2, piece, 2 * feat), BF16),
            pltpu.VMEM((4, 2, piece, 2 * feat), BF16),
            pltpu.VMEM((RING - 1, piece, 2 * feat), BF16),
            pltpu.VMEM((2, half, feat), F32),
            dma((8,)),
            dma((80,)),
            dma((10,)),
            dma((10,)),
            dma((10,)),
            dma((4, 2)),
            dma((4, 2)),
            dma((4,)),
            dma((3, 2)),
            dma((5, Y - 1)),
            dma((RING - 1,)),
            pltpu.SemaphoreType.REGULAR((3,)),
        ],
        compiler_params=pltpu.CompilerParams(
            collective_id=0, has_side_effects=True, vmem_limit_bytes=67043328
        ),
        name="attention_backward",
    )(
        query,
        key.reshape(Y, 2, piece, feat),
        value.reshape(Y, 2, piece, feat),
        output, out_grad, lse, block_order,
    )
    return pl.pallas_call(
        finish,
        out_shape=(
            jax.ShapeDtypeStruct((1, rows, feat), F32),
            jax.ShapeDtypeStruct((piece, feat), F32),
            jax.ShapeDtypeStruct((piece, feat), F32),
        ),
        in_specs=[any_space] * 2,
        out_specs=(any_space,) * 3,
        scratch_shapes=[
            pltpu.VMEM((2, half, feat), F32),
            pltpu.VMEM((2, piece, feat), F32),
            dma((4,)),
            dma((4,)),
        ],
        compiler_params=pltpu.CompilerParams(vmem_limit_bytes=67043328),
        name="finish",
    )(dq, dkv)


def solution(mesh):
    in_specs = (
        P("head", "blk", None),
        P("blk", None),
        P("blk", None),
        P("head", "blk", None),
        P("head", "blk", None),
        P("head", "blk"),
        P(),
    )
    out_specs = (P("head", "blk", None), P(("blk", "head"), None), P(("blk", "head"), None))
    return jax.shard_map(
        on_device, mesh=mesh, in_specs=in_specs, out_specs=out_specs, check_vma=False
    )
```

```python
import jax
import jax.numpy as jnp
from jax import lax
from jax.experimental import pallas as pl
from jax.experimental.pallas import tpu as pltpu
from jax.sharding import PartitionSpec as P

F32 = jnp.float32
BF16 = jnp.bfloat16
MESH = pl.DeviceIdType.MESH
LOG2E = 1.4426950408889634
DEAD = 1.0e9
PAIR = (0, 0, 1, 1, 0, 2, 2, 1, 3, 3, 2, 3, 3, 2)
KEYS = (0, 1, 0, 1, 2, 0, 1, 2, 0, 1, 2, 2, 3, 3)
X, Z, C, Y = 4, 4, 2, 4
RING = 8


def dot(left, right, left_dim, right_dim):
    return lax.dot_general(
        left, right, (((left_dim,), (right_dim,)), ((), ())), preferred_element_type=F32
    )


def kernel(
    q_hbm, k_hbm, v_hbm, o_hbm, g_hbm, l_hbm, order,
    dq_out, dkv_out,
    qb, gb, sb, kb, vb, ob, lb,
    dq_acc, dk_acc, dv_acc, core_in, x_out, x_in,
    y_out, y_own, y_in, z_out, z_in, dq_rows,
    load_sem, send_sem, q_sem, g_sem, s_sem, k_sem, v_sem, core_sem, x_sem, y_sem, z_sem, round_sem,
):
    rows, feat = ob.shape
    half, piece = rows // 2, rows // RING
    scale = feat ** -0.5
    blk = lax.axis_index("blk")
    head = lax.axis_index("head")
    core = blk % C
    zlo = (blk // C) % Z
    x = blk // (C * Z)
    zhi = head % 2
    y = head // 2
    ring = zhi * Z + zlo

    def at(dx=0, dc=0):
        return {"blk": (((x + dx) % X) * Z + zlo) * C + (core + dc) % C, "head": head}

    def at_y(dy):
        return {"blk": blk, "head": ((y + dy) % Y) * 2 + zhi}

    def at_ring(dz):
        there = (ring + dz) % RING
        return {"blk": (x * Z + there % Z) * C + core, "head": y * 2 + there // Z}

    beside = [at(dx=1), at(dx=3), at_y(1), at_y(3), at_ring(1), at_ring(7)]
    greeted = [at(dc=1)] + beside
    barrier = pltpu.get_barrier_semaphore()
    for device in greeted:
        pl.semaphore_signal(barrier, inc=1, device_id=device, device_id_type=MESH)

    loads = []
    own = pl.ds(0, rows)
    for src, dst in (
        (g_hbm.at[0], gb.at[0, own]), (o_hbm.at[0], ob), (l_hbm, lb), (q_hbm.at[0], qb.at[0, own]),
        (k_hbm.at[:, 0], kb.at[0, 0]), (v_hbm.at[:, 0], vb.at[0, 0]),
        (k_hbm.at[:, 1], kb.at[0, 1]), (v_hbm.at[:, 1], vb.at[0, 1]),
    ):
        loads.append(pltpu.make_async_copy(src, dst, load_sem.at[len(loads)]))
        loads[-1].start()

    sends = []

    def remote(src, dst, recv, device):
        copy = pltpu.make_async_remote_copy(
            src_ref=src, dst_ref=dst, send_sem=send_sem.at[len(sends)], recv_sem=recv,
            device_id=device, device_id_type=MESH,
        )
        sends.append(copy)
        return copy

    def landed(dst, recv):
        pltpu.make_async_remote_copy(
            src_ref=dst, dst_ref=dst, send_sem=send_sem.at[0], recv_sem=recv,
            device_id=at(dc=1), device_id_type=MESH,
        ).wait_recv()

    def send_round(i):
        for device in (beside, beside[4:], beside[4:])[i]:
            pl.semaphore_signal(round_sem.at[i], inc=1, device_id=device, device_id_type=MESH)

    def wait_round(i):
        pl.semaphore_wait(round_sem.at[i], (6, 2, 2)[i])

    def start(copies):
        for copy in copies:
            copy.start()

    def part(buf, place):
        p, first, count = place
        return buf.at[p, pl.ds(first, count)]

    def stat(place):
        p, first, count = place
        return sb.at[p, :, pl.ds(first, count)]

    def pass_q(src, dst, i, device):
        return remote(part(qb, src), part(qb, dst), q_sem.at[i], device)

    def pass_g(src, dst, i, device):
        return remote(part(gb, src), part(gb, dst), g_sem.at[i], device)

    def pass_s(src, dst, i, device):
        return remote(stat(src), stat(dst), s_sem.at[i], device)

    def pass_all(src, dst, i, device):
        return [f(src, dst, i, device) for f in (pass_q, pass_g, pass_s)]

    def got(place, i):
        landed(part(qb, place), q_sem.at[i])
        landed(part(gb, place), g_sem.at[i])
        landed(stat(place), s_sem.at[i])

    def got_keys(r, h):
        landed(kb.at[r, h], k_sem.at[r, h])
        landed(vb.at[r, h], v_sem.at[r, h])

    to_core = pass_all((0, 0, rows), (0, rows, rows), 0, at(dc=1))
    waves, keys_out, forward, relay_x, relay_z = [], [], [], [], []
    for w in (0, 1):
        mine, p, i = (0, w * half, half), 1 + w, 3 * w + 1
        right = pass_all(mine, (p, half, half), i + 1, at(dx=1))
        left = pass_all(mine, (p, 0, half), i, at(dx=3))
        waves.append((right, left))
        keys_out.append([
            remote(buf.at[0, w], buf.at[p, h], sem.at[p, h], at_ring(dz))
            for buf, sem in ((kb, k_sem), (vb, v_sem)) for h, dz in ((1, 1), (0, 7))
        ])
        forward.append(pass_all((p, 0, rows), (p, rows, rows), i + 2, at(dc=1)))
        far = (3, w * half, half)
        relay_x.append([
            pass_q((p, 0, half), far, 7 + w, at(dx=3)),
            pass_g((p, half, half), far, 7 + w, at(dx=1)),
            pass_s((p, 0, half), far, 7 + w, at(dx=3)),
        ])
        relay_z.append([
            remote(buf.at[p, w], buf.at[3, w], sem.at[3, w], at_ring((7, 1)[w]))
            for buf, sem in ((kb, k_sem), (vb, v_sem))
        ])
    forward_far = pass_all((3, 0, rows), (3, rows, rows), 9, at(dc=1))
    dq_core = [remote(dq_acc.at[p, 1], core_in.at[p], core_sem.at[p], at(dc=1)) for p in range(4)]
    dq_x = [None] + [
        [remote(x_out.at[w, i], x_in.at[2 * i, w], x_sem.at[2 * i, w], at(dx=(1, 3)[i])) for i in (0, 1)]
        for w in (0, 1)
    ] + [[remote(x_out.at[2, w], x_in.at[1, w], x_sem.at[1, w], at(dx=2)) for w in (0, 1)]]
    kv_y = [
        [remote(y_out.at[r, (y + i) % Y], y_in.at[r, i - 1], y_sem.at[r, i - 1], at_y(i)) for i in (2, 1, 3)]
        for r in range(3)
    ]
    kv_y_last = [
        [
            remote(
                y_out.at[3, (y + i) % Y, h], y_in.at[3, i - 1, h], y_sem.at[3 + h, i - 1], at_y(i)
            )
            for i in (2, 1, 3)
        ]
        for h in (0, 1)
    ]
    kv_z = [[remote(z_out.at[0, 1 - zhi], z_in.at[Z - 1], z_sem.at[Z - 1], at_ring(Z))]]
    for r, targets in ((1, ((1, 0), (3, 0))), (2, ((1, 1), (3, 1))), (3, ((2, 0), (2, 1)))):
        kv_z.append([])
        for h, (dz, side) in enumerate(targets):
            ahead = (side * Z + (zlo + dz) % Z - ring + RING) % RING
            kv_z[r].append(
                remote(z_out.at[r, h], z_in.at[ahead - 1], z_sem.at[ahead - 1], at_ring(ahead))
            )

    for i in (0, 1, 2):
        loads[i].wait()
    delta = jnp.sum(jnp.transpose(gb[0, own].astype(F32) * ob[...].astype(F32)), axis=0, keepdims=True)
    sb[0, 0:1, own] = lb[...] * LOG2E
    sb[0, 1:2, own] = delta
    for i in range(3, 8):
        loads[i].wait()
    pl.semaphore_wait(barrier, len(greeted))

    def send_wave(w):
        right, left = waves[w]
        start([right[0], left[0], right[1], left[1]])
        start(keys_out[w])
        start([right[2], left[2]])

    start(to_core[:2])
    send_wave(0)
    start([to_core[2]])
    dq_acc[...] = jnp.zeros_like(dq_acc)
    send_round(0)
    dk_acc[...] = jnp.zeros_like(dk_acc)
    dv_acc[...] = jnp.zeros_like(dv_acc)

    def block(dx, dc, dz, b):
        return order[2 * (((x + dx) % X * Z + (zlo + dz) % Z) * C + (core + dc) % C) + b]

    def grads(kv_at, keys, vals, q_rows, g_rows, probs, d_row):
        dprobs = dot(vals, g_rows, 1, 1)
        dscores = (probs * (dprobs - d_row)).astype(BF16)
        shape = dv_acc.at[kv_at].shape
        dv_acc[kv_at] += dot(probs.astype(BF16), g_rows, 1, 0).reshape(shape)
        dk_acc[kv_at] += dot(dscores, q_rows, 1, 0).reshape(shape)
        return dot(keys, dscores, 0, 0)

    def biased(l_row, q_blocks, k_block):
        parts = []
        for i, q_block in enumerate(q_blocks):
            dead = jnp.where(q_block > k_block, 0.0, DEAD)
            parts.append(l_row[:, i * half : (i + 1) * half] + dead)
        return jnp.concatenate(parts, axis=1)

    def tile(kv_at, p, first, count, q_blocks, k_blocks):
        cols = pl.ds(first * rows, count * rows)
        keys, vals = kb[kv_at].reshape(-1, feat), vb[kv_at].reshape(-1, feat)
        q_rows, g_rows = qb[p, cols], gb[p, cols]
        l_row, d_row = sb[p, 0:1, cols], sb[p, 1:2, cols]
        lows = jnp.stack([biased(l_row, q_blocks, b) for b in k_blocks])
        scores = dot(keys, q_rows, 1, 1).reshape(len(k_blocks), half // 2, count * rows)
        probs = jnp.exp2(scores * (scale * LOG2E) - lows).reshape(-1, count * rows)
        part_q = grads(kv_at, keys, vals, q_rows, g_rows, probs, d_row)
        for i in range(count):
            dq_acc[p, first + i] += part_q[:, i * rows : (i + 1) * rows]

    own_blocks = [block(0, 0, 0, b) for b in (0, 1)]
    q_rows, g_rows = qb[0, own], gb[0, own]
    at_row = lax.broadcasted_iota(jnp.int32, (rows, 1), 0)
    at_col = lax.broadcasted_iota(jnp.int32, (1, rows), 1)
    quarter = at_row % half // piece
    k_off = quarter % 2 * (2 * piece) + at_row // half * piece + at_row % piece
    k_pos = jnp.where(quarter < 2, own_blocks[0], own_blocks[1]) * half + k_off
    q_pos = jnp.where(at_col < half, own_blocks[0], own_blocks[1]) * half + at_col % half
    keys, vals = kb[0].reshape(rows, feat), vb[0].reshape(rows, feat)
    scores = dot(keys, q_rows, 1, 1)
    probs = jnp.where(
        q_pos >= k_pos, jnp.exp2(scores * (scale * LOG2E) - sb[0, 0:1, own]), 0.0
    )
    dq_acc[0, 0] += grads((0,), keys, vals, q_rows, g_rows, probs, sb[0, 1:2, own])

    got((0, rows, rows), 0)
    tile((0,), 0, 1, 1, [block(0, 1, 0, b) for b in (0, 1)], own_blocks * 2)
    send_wave(1)

    def stage(r, h):
        y_out[r, :, h, :, :feat] = dk_acc[r, h].astype(BF16)
        y_out[r, :, h, :, feat:] = dv_acc[r, h].astype(BF16)
        y_own[r, h, :, :feat] = dk_acc[r, h, y]
        y_own[r, h, :, feat:] = dv_acc[r, h, y]

    def stage_row(r):
        stage(r, 0)
        stage(r, 1)

    def sum_y(r):
        total = y_own[r]
        for i in range(Y - 1):
            landed(y_in.at[r, i], y_sem.at[r, i])
            total = total + y_in[r, i].astype(F32)
        z_out[r] = total.astype(BF16)
        if r == 0:
            y_own[0] = total

    def sum_y_last(h):
        total = y_own[3, h]
        for i in range(Y - 1):
            landed(y_in.at[3, i, h], y_sem.at[3 + h, i])
            total = total + y_in[3, i, h].astype(F32)
        z_out[3, h] = total.astype(BF16)

    def join_core(p):
        landed(core_in.at[p], core_sem.at[p])
        total = (dq_acc[p, 0] + core_in[p]).astype(BF16)
        x_out[p - 1, 0] = total[:, :half]
        x_out[p - 1, 1] = total[:, half:]

    before = {
        1: lambda: (
            got((1, 0, half), 1), got((1, half, half), 2), start(forward[0]), start(relay_x[0]),
            got_keys(1, 0), start(relay_z[0]), got_keys(1, 1),
        ),
        2: lambda: got((1, rows, rows), 3),
        3: lambda: (
            got((2, 0, half), 4), got((2, half, half), 5), start(forward[1]), start(relay_x[1]),
        ),
        4: lambda: (wait_round(0), send_round(1), got_keys(2, 1), start(relay_z[1]), got_keys(2, 0)),
        5: lambda: (wait_round(1), send_round(2), got((2, rows, rows), 6)),
        6: lambda: (wait_round(2), got((3, 0, half), 7), got((3, half, half), 8), start(forward_far)),
        8: lambda: got((3, rows, rows), 9),
        12: lambda: (got_keys(3, 0), got_keys(3, 1)),
    }
    after = {
        8: lambda: stage_row(0),
        9: lambda: (start(kv_y[0]), stage_row(1)),
        10: lambda: start(kv_y[1]),
        11: lambda: stage_row(2),
        12: lambda: (start(kv_y[2]), dq_core[3].start()),
        13: lambda: (dq_core[2].start(), sum_y(0)),
    }
    after_half = {
        0: lambda: (start(kv_z[0]), join_core(3)),
        1: lambda: (start(dq_x[3]), stage(3, 0)),
        2: lambda: (dq_core[1].start(), start(kv_y_last[0]), join_core(2)),
        3: lambda: (start(dq_x[2]), dq_core[0].start(), stage(3, 1)),
    }

    def chosen(t, table):
        out = jnp.int32(table[1])
        for i in range(2, len(table)):
            out = jnp.where(t == i, table[i], out)
        return out

    def pair_blocks(p):
        near = (p + 1) // 2
        mid = near % 2
        return [
            block((near, 4 - near)[j % 2], j // 2, 0, j % 2 * (1 - mid) + mid * (p - 1)) for j in range(4)
        ]

    def step(t, carry):
        p, r = chosen(t, PAIR), chosen(t, KEYS)
        for i, action in before.items():
            @pl.when(t == i)
            def _():
                action()

        far = (r + 1) // 2
        k_blocks = [block(0, 0, (far, 4 - far)[h], b) for h in (0, 1) for b in (0, 1)]
        tile((r,), p, 0, 2, pair_blocks(p), k_blocks)

        for i, action in after.items():
            @pl.when(t == i)
            def _():
                action()

        return carry

    lax.fori_loop(1, len(PAIR), step, 0)

    def half_step(t, carry):
        p, h = 1 - t % 2, t // 2
        tile((3, h), p, 0, 2, pair_blocks(p), [block(0, 0, 2, b) for b in (0, 1)])
        for i, action in after_half.items():
            @pl.when(t == i)
            def _():
                action()

        return carry

    lax.fori_loop(0, 4, half_step, 0)

    sum_y(1)
    start(kv_y_last[1])
    start(kv_z[1])
    join_core(1)
    sum_y(2)
    start(dq_x[1])
    start(kv_z[2])
    sum_y_last(0)
    landed(core_in.at[0], core_sem.at[0])
    dq_acc[0, 0, :, :half] += core_in[0, :, :half]
    start(kv_z[3][:1])
    sum_y_last(1)
    dq_acc[0, 0, :, half:] += core_in[0, :, half:]
    start(kv_z[3][1:])
    for w in (0, 1):
        side = dq_acc[0, 0, :, w * half : (w + 1) * half]
        for i in (1, 0, 2):
            landed(x_in.at[i, w], x_sem.at[i, w])
            side = side + x_in[i, w].astype(F32)
        dq_rows[w] = jnp.transpose(side * scale)
    total = y_own[0, zhi]
    for i in (4, 1, 5, 3, 7):
        landed(z_in.at[i - 1], z_sem.at[i - 1])
        total = total + z_in[i - 1].astype(F32)
    dq_leave = pltpu.make_async_copy(dq_rows, dq_out.at[0], load_sem.at[0])
    dq_leave.start()
    for i in (2, 6):
        landed(z_in.at[i - 1], z_sem.at[i - 1])
        total = total + z_in[i - 1].astype(F32)
    dkv_out[0] = total[:, :feat] * scale
    dkv_out[1] = total[:, feat:]
    dq_leave.wait()
    for copy in sends:
        copy.wait_send()


def finish(dq_in, dkv_in, dq_out, dk_out, dv_out, held, held_kv, in_sem, out_sem):
    half = held.shape[1]
    moves = [
        (dq_in.at[0, w], held.at[w], dq_out.at[0, pl.ds(w * half, half)]) for w in (0, 1)
    ] + [(dkv_in.at[i], held_kv.at[i], out) for i, out in enumerate((dk_out, dv_out))]
    arrivals = [
        pltpu.make_async_copy(src, at, in_sem.at[i]) for i, (src, at, _) in enumerate(moves)
    ]
    leaves = [
        pltpu.make_async_copy(at, dst, out_sem.at[i]) for i, (_, at, dst) in enumerate(moves)
    ]
    for copy in arrivals:
        copy.start()
    for arrival, leave in zip(arrivals, leaves):
        arrival.wait()
        leave.start()
    for leave in leaves:
        leave.wait()


def on_device(query, key, value, output, out_grad, lse, block_order):
    rows, feat = key.shape
    half, piece = rows // 2, rows // RING
    any_space = pl.BlockSpec(memory_space=pl.ANY)
    vmem = pl.BlockSpec(memory_space=pltpu.VMEM)
    dma = pltpu.SemaphoreType.DMA
    dq, dkv = pl.pallas_call(
        kernel,
        out_shape=(
            jax.ShapeDtypeStruct((1, 2, half, feat), F32),
            jax.ShapeDtypeStruct((2, piece, feat), F32),
        ),
        in_specs=[any_space] * 6 + [pl.BlockSpec(memory_space=pltpu.SMEM)],
        out_specs=(any_space, vmem),
        scratch_shapes=[
            pltpu.VMEM((4, 2 * rows, feat), BF16),
            pltpu.VMEM((4, 2 * rows, feat), BF16),
            pltpu.VMEM((4, 2, 2 * rows), F32),
            pltpu.VMEM((4, 2, Y, piece, feat), BF16),
            pltpu.VMEM((4, 2, Y, piece, feat), BF16),
            pltpu.VMEM((rows, feat), BF16),
            pltpu.VMEM((1, rows), F32),
            pltpu.VMEM((4, 2, feat, rows), F32),
            pltpu.VMEM((4, 2, Y, piece, feat), F32),
            pltpu.VMEM((4, 2, Y, piece, feat), F32),
            pltpu.VMEM((4, feat, rows), F32),
            pltpu.VMEM((3, 2, feat, half), BF16),
            pltpu.VMEM((3, 2, feat, half), BF16),
            pltpu.VMEM((4, Y, 2, piece, 2 * feat), BF16),
            pltpu.VMEM((4, 2, piece, 2 * feat), F32),
            pltpu.VMEM((4, Y - 1, 2, piece, 2 * feat), BF16),
            pltpu.VMEM((4, 2, piece, 2 * feat), BF16),
            pltpu.VMEM((RING - 1, piece, 2 * feat), BF16),
            pltpu.VMEM((2, half, feat), F32),
            dma((8,)),
            dma((80,)),
            dma((10,)),
            dma((10,)),
            dma((10,)),
            dma((4, 2)),
            dma((4, 2)),
            dma((4,)),
            dma((3, 2)),
            dma((5, Y - 1)),
            dma((RING - 1,)),
            pltpu.SemaphoreType.REGULAR((3,)),
        ],
        compiler_params=pltpu.CompilerParams(
            collective_id=0, has_side_effects=True, vmem_limit_bytes=67043328
        ),
        name="attention_backward",
    )(
        query,
        key.reshape(Y, 2, piece, feat),
        value.reshape(Y, 2, piece, feat),
        output, out_grad, lse, block_order,
    )
    return pl.pallas_call(
        finish,
        out_shape=(
            jax.ShapeDtypeStruct((1, rows, feat), F32),
            jax.ShapeDtypeStruct((piece, feat), F32),
            jax.ShapeDtypeStruct((piece, feat), F32),
        ),
        in_specs=[any_space] * 2,
        out_specs=(any_space,) * 3,
        scratch_shapes=[
            pltpu.VMEM((2, half, feat), F32),
            pltpu.VMEM((2, piece, feat), F32),
            dma((4,)),
            dma((4,)),
        ],
        compiler_params=pltpu.CompilerParams(vmem_limit_bytes=67043328),
        name="finish",
    )(dq, dkv)


def solution(mesh):
    in_specs = (
        P("head", "blk", None),
        P("blk", None),
        P("blk", None),
        P("head", "blk", None),
        P("head", "blk", None),
        P("head", "blk"),
        P(),
    )
    out_specs = (P("head", "blk", None), P(("blk", "head"), None), P(("blk", "head"), None))
    return jax.shard_map(
        on_device, mesh=mesh, in_specs=in_specs, out_specs=out_specs, check_vma=False
    )
```

```python
import jax
import jax.numpy as jnp
from jax import lax
from jax.experimental import pallas as pl
from jax.experimental.pallas import tpu as pltpu
from jax.sharding import PartitionSpec as P

F32 = jnp.float32
BF16 = jnp.bfloat16
MESH = pl.DeviceIdType.MESH
LOG2E = 1.4426950408889634
DEAD = 1.0e9
PAIR = (0, 0, 1, 1, 0, 2, 2, 1, 3, 3, 2, 3, 3, 2)
KEYS = (0, 1, 0, 1, 2, 0, 1, 2, 0, 1, 2, 2, 3, 3)
X, Z, C, Y = 4, 4, 2, 4
RING = 8


def dot(left, right, left_dim, right_dim):
    return lax.dot_general(
        left, right, (((left_dim,), (right_dim,)), ((), ())), preferred_element_type=F32
    )


def kernel(
    q_hbm, k_hbm, v_hbm, o_hbm, g_hbm, l_hbm, order,
    dq_out, dkv_out,
    qb, gb, sb, kb, vb, ob, lb,
    dq_acc, dk_acc, dv_acc, core_in, x_out, x_in,
    y_out, y_own, y_in, z_out, z_in, dq_rows,
    load_sem, send_sem, q_sem, g_sem, s_sem, k_sem, v_sem, core_sem, x_sem, y_sem, z_sem, round_sem,
):
    rows, feat = ob.shape
    half, piece = rows // 2, rows // RING
    scale = feat ** -0.5
    blk = lax.axis_index("blk")
    head = lax.axis_index("head")
    core = blk % C
    zlo = (blk // C) % Z
    x = blk // (C * Z)
    zhi = head % 2
    y = head // 2
    ring = zhi * Z + zlo

    def at(dx=0, dc=0):
        return {"blk": (((x + dx) % X) * Z + zlo) * C + (core + dc) % C, "head": head}

    def at_y(dy):
        return {"blk": blk, "head": ((y + dy) % Y) * 2 + zhi}

    def at_ring(dz):
        there = (ring + dz) % RING
        return {"blk": (x * Z + there % Z) * C + core, "head": y * 2 + there // Z}

    beside = [at(dx=1), at(dx=3), at_y(1), at_y(3), at_ring(1), at_ring(7)]
    greeted = [at(dc=1)] + beside
    barrier = pltpu.get_barrier_semaphore()
    for device in greeted:
        pl.semaphore_signal(barrier, inc=1, device_id=device, device_id_type=MESH)

    loads = []
    own = pl.ds(0, rows)
    for src, dst in (
        (g_hbm.at[0], gb.at[0, own]), (o_hbm.at[0], ob), (l_hbm, lb), (q_hbm.at[0], qb.at[0, own]),
        (k_hbm.at[:, 0], kb.at[0, 0]), (v_hbm.at[:, 0], vb.at[0, 0]),
        (k_hbm.at[:, 1], kb.at[0, 1]), (v_hbm.at[:, 1], vb.at[0, 1]),
    ):
        loads.append(pltpu.make_async_copy(src, dst, load_sem.at[len(loads)]))
        loads[-1].start()

    sends = []

    def remote(src, dst, recv, device):
        copy = pltpu.make_async_remote_copy(
            src_ref=src, dst_ref=dst, send_sem=send_sem.at[len(sends)], recv_sem=recv,
            device_id=device, device_id_type=MESH,
        )
        sends.append(copy)
        return copy

    def landed(dst, recv):
        pltpu.make_async_remote_copy(
            src_ref=dst, dst_ref=dst, send_sem=send_sem.at[0], recv_sem=recv,
            device_id=at(dc=1), device_id_type=MESH,
        ).wait_recv()

    def send_round(i):
        for device in (beside, beside[4:], beside[4:])[i]:
            pl.semaphore_signal(round_sem.at[i], inc=1, device_id=device, device_id_type=MESH)

    def wait_round(i):
        pl.semaphore_wait(round_sem.at[i], (6, 2, 2)[i])

    def start(copies):
        for copy in copies:
            copy.start()

    def part(buf, place):
        p, first, count = place
        return buf.at[p, pl.ds(first, count)]

    def stat(place):
        p, first, count = place
        return sb.at[p, :, pl.ds(first, count)]

    def pass_q(src, dst, i, device):
        return remote(part(qb, src), part(qb, dst), q_sem.at[i], device)

    def pass_g(src, dst, i, device):
        return remote(part(gb, src), part(gb, dst), g_sem.at[i], device)

    def pass_s(src, dst, i, device):
        return remote(stat(src), stat(dst), s_sem.at[i], device)

    def pass_all(src, dst, i, device):
        return [f(src, dst, i, device) for f in (pass_q, pass_g, pass_s)]

    def got(place, i):
        landed(part(qb, place), q_sem.at[i])
        landed(part(gb, place), g_sem.at[i])
        landed(stat(place), s_sem.at[i])

    def got_keys(r, h):
        landed(kb.at[r, h], k_sem.at[r, h])
        landed(vb.at[r, h], v_sem.at[r, h])

    to_core = pass_all((0, 0, rows), (0, rows, rows), 0, at(dc=1))
    waves, keys_out, forward, relay_x, relay_z = [], [], [], [], []
    for w in (0, 1):
        mine, p, i = (0, w * half, half), 1 + w, 3 * w + 1
        right = pass_all(mine, (p, half, half), i + 1, at(dx=1))
        left = pass_all(mine, (p, 0, half), i, at(dx=3))
        waves.append((right, left))
        keys_out.append([
            remote(buf.at[0, w], buf.at[p, h], sem.at[p, h], at_ring(dz))
            for buf, sem in ((kb, k_sem), (vb, v_sem)) for h, dz in ((1, 1), (0, 7))
        ])
        forward.append(pass_all((p, 0, rows), (p, rows, rows), i + 2, at(dc=1)))
        far = (3, w * half, half)
        relay_x.append([
            pass_q((p, 0, half), far, 7 + w, at(dx=3)),
            pass_g((p, half, half), far, 7 + w, at(dx=1)),
            pass_s((p, 0, half), far, 7 + w, at(dx=3)),
        ])
        relay_z.append([
            remote(buf.at[p, w], buf.at[3, w], sem.at[3, w], at_ring((7, 1)[w]))
            for buf, sem in ((kb, k_sem), (vb, v_sem))
        ])
    forward_far = pass_all((3, 0, rows), (3, rows, rows), 9, at(dc=1))
    dq_core = [remote(dq_acc.at[p, 1], core_in.at[p], core_sem.at[p], at(dc=1)) for p in range(4)]
    dq_x = [None] + [
        [remote(x_out.at[w, i], x_in.at[2 * i, w], x_sem.at[2 * i, w], at(dx=(1, 3)[i])) for i in (0, 1)]
        for w in (0, 1)
    ] + [[remote(x_out.at[2, w], x_in.at[1, w], x_sem.at[1, w], at(dx=2)) for w in (0, 1)]]
    kv_y = [
        [remote(y_out.at[r, (y + i) % Y], y_in.at[r, i - 1], y_sem.at[r, i - 1], at_y(i)) for i in (2, 1, 3)]
        for r in range(3)
    ]
    kv_y_last = [
        [
            remote(
                y_out.at[3, (y + i) % Y, h], y_in.at[3, i - 1, h], y_sem.at[3 + h, i - 1], at_y(i)
            )
            for i in (2, 1, 3)
        ]
        for h in (0, 1)
    ]
    kv_z = [[remote(z_out.at[0, 1 - zhi], z_in.at[Z - 1], z_sem.at[Z - 1], at_ring(Z))]]
    for r, targets in ((1, ((1, 0), (3, 0))), (2, ((1, 1), (3, 1))), (3, ((2, 0), (2, 1)))):
        kv_z.append([])
        for h, (dz, side) in enumerate(targets):
            ahead = (side * Z + (zlo + dz) % Z - ring + RING) % RING
            kv_z[r].append(
                remote(z_out.at[r, h], z_in.at[ahead - 1], z_sem.at[ahead - 1], at_ring(ahead))
            )

    for i in (0, 1, 2):
        loads[i].wait()
    delta = jnp.sum(jnp.transpose(gb[0, own].astype(F32) * ob[...].astype(F32)), axis=0, keepdims=True)
    sb[0, 0:1, own] = lb[...] * LOG2E
    sb[0, 1:2, own] = delta
    for i in range(3, 8):
        loads[i].wait()
    pl.semaphore_wait(barrier, len(greeted))

    def send_wave(w):
        right, left = waves[w]
        start([right[0], left[0], right[1], left[1]])
        start(keys_out[w])
        start([right[2], left[2]])

    start(to_core[:2])
    send_wave(0)
    start([to_core[2]])
    dq_acc[...] = jnp.zeros_like(dq_acc)
    send_round(0)
    dk_acc[...] = jnp.zeros_like(dk_acc)
    dv_acc[...] = jnp.zeros_like(dv_acc)

    def block(dx, dc, dz, b):
        return order[2 * (((x + dx) % X * Z + (zlo + dz) % Z) * C + (core + dc) % C) + b]

    def grads(kv_at, keys, vals, q_rows, g_rows, probs, d_row):
        dprobs = dot(vals, g_rows, 1, 1)
        dscores = (probs * (dprobs - d_row)).astype(BF16)
        shape = dv_acc.at[kv_at].shape
        dv_acc[kv_at] += dot(probs.astype(BF16), g_rows, 1, 0).reshape(shape)
        dk_acc[kv_at] += dot(dscores, q_rows, 1, 0).reshape(shape)
        return dot(keys, dscores, 0, 0)

    def biased(l_row, q_blocks, k_block):
        parts = []
        for i, q_block in enumerate(q_blocks):
            dead = jnp.where(q_block > k_block, 0.0, DEAD)
            parts.append(l_row[:, i * half : (i + 1) * half] + dead)
        return jnp.concatenate(parts, axis=1)

    def tile(kv_at, p, first, count, q_blocks, k_blocks):
        cols = pl.ds(first * rows, count * rows)
        keys, vals = kb[kv_at].reshape(-1, feat), vb[kv_at].reshape(-1, feat)
        q_rows, g_rows = qb[p, cols], gb[p, cols]
        l_row, d_row = sb[p, 0:1, cols], sb[p, 1:2, cols]
        lows = jnp.stack([biased(l_row, q_blocks, b) for b in k_blocks])
        scores = dot(keys, q_rows, 1, 1).reshape(len(k_blocks), half // 2, count * rows)
        probs = jnp.exp2(scores * (scale * LOG2E) - lows).reshape(-1, count * rows)
        part_q = grads(kv_at, keys, vals, q_rows, g_rows, probs, d_row)
        for i in range(count):
            dq_acc[p, first + i] += part_q[:, i * rows : (i + 1) * rows]

    own_blocks = [block(0, 0, 0, b) for b in (0, 1)]
    q_rows, g_rows = qb[0, own], gb[0, own]
    at_row = lax.broadcasted_iota(jnp.int32, (rows, 1), 0)
    at_col = lax.broadcasted_iota(jnp.int32, (1, rows), 1)
    quarter = at_row % half // piece
    k_off = quarter % 2 * (2 * piece) + at_row // half * piece + at_row % piece
    k_pos = jnp.where(quarter < 2, own_blocks[0], own_blocks[1]) * half + k_off
    q_pos = jnp.where(at_col < half, own_blocks[0], own_blocks[1]) * half + at_col % half
    keys, vals = kb[0].reshape(rows, feat), vb[0].reshape(rows, feat)
    scores = dot(keys, q_rows, 1, 1)
    probs = jnp.where(
        q_pos >= k_pos, jnp.exp2(scores * (scale * LOG2E) - sb[0, 0:1, own]), 0.0
    )
    dq_acc[0, 0] += grads((0,), keys, vals, q_rows, g_rows, probs, sb[0, 1:2, own])

    got((0, rows, rows), 0)
    tile((0,), 0, 1, 1, [block(0, 1, 0, b) for b in (0, 1)], own_blocks * 2)
    send_wave(1)

    def stage(r, h):
        y_out[r, :, h, :, :feat] = dk_acc[r, h].astype(BF16)
        y_out[r, :, h, :, feat:] = dv_acc[r, h].astype(BF16)
        y_own[r, h, :, :feat] = dk_acc[r, h, y]
        y_own[r, h, :, feat:] = dv_acc[r, h, y]

    def stage_row(r):
        stage(r, 0)
        stage(r, 1)

    def sum_y(r):
        total = y_own[r]
        for i in range(Y - 1):
            landed(y_in.at[r, i], y_sem.at[r, i])
            total = total + y_in[r, i].astype(F32)
        z_out[r] = total.astype(BF16)
        if r == 0:
            y_own[0] = total

    def sum_y_last(h):
        total = y_own[3, h]
        for i in range(Y - 1):
            landed(y_in.at[3, i, h], y_sem.at[3 + h, i])
            total = total + y_in[3, i, h].astype(F32)
        z_out[3, h] = total.astype(BF16)

    def join_core(p):
        landed(core_in.at[p], core_sem.at[p])
        total = (dq_acc[p, 0] + core_in[p]).astype(BF16)
        x_out[p - 1, 0] = total[:, :half]
        x_out[p - 1, 1] = total[:, half:]

    before = {
        1: lambda: (
            got((1, 0, half), 1), got((1, half, half), 2), start(forward[0]), start(relay_x[0]),
            got_keys(1, 0), start(relay_z[0]), got_keys(1, 1),
        ),
        2: lambda: got((1, rows, rows), 3),
        3: lambda: (
            got((2, 0, half), 4), got((2, half, half), 5), start(forward[1]), start(relay_x[1]),
        ),
        4: lambda: (wait_round(0), send_round(1), got_keys(2, 1), start(relay_z[1]), got_keys(2, 0)),
        5: lambda: (wait_round(1), send_round(2), got((2, rows, rows), 6)),
        6: lambda: (wait_round(2), got((3, 0, half), 7), got((3, half, half), 8), start(forward_far)),
        8: lambda: got((3, rows, rows), 9),
        12: lambda: (got_keys(3, 0), got_keys(3, 1)),
    }
    after = {
        8: lambda: stage_row(0),
        9: lambda: (start(kv_y[0]), stage_row(1)),
        10: lambda: start(kv_y[1]),
        11: lambda: stage_row(2),
        12: lambda: (start(kv_y[2]), dq_core[3].start()),
        13: lambda: (dq_core[2].start(), sum_y(0)),
    }
    after_half = {
        0: lambda: (start(kv_z[0]), join_core(3)),
        1: lambda: (start(dq_x[3]), stage(3, 0)),
        2: lambda: (dq_core[1].start(), start(kv_y_last[0]), join_core(2)),
        3: lambda: (start(dq_x[2]), dq_core[0].start(), stage(3, 1)),
    }

    def chosen(t, table):
        out = jnp.int32(table[1])
        for i in range(2, len(table)):
            out = jnp.where(t == i, table[i], out)
        return out

    def pair_blocks(p):
        near = (p + 1) // 2
        mid = near % 2
        return [
            block((near, 4 - near)[j % 2], j // 2, 0, j % 2 * (1 - mid) + mid * (p - 1)) for j in range(4)
        ]

    def step(t, carry):
        p, r = chosen(t, PAIR), chosen(t, KEYS)
        for i, action in before.items():
            @pl.when(t == i)
            def _():
                action()

        far = (r + 1) // 2
        k_blocks = [block(0, 0, (far, 4 - far)[h], b) for h in (0, 1) for b in (0, 1)]
        tile((r,), p, 0, 2, pair_blocks(p), k_blocks)

        for i, action in after.items():
            @pl.when(t == i)
            def _():
                action()

        return carry

    lax.fori_loop(1, len(PAIR), step, 0)

    def half_step(t, carry):
        p, h = 1 - t % 2, t // 2
        tile((3, h), p, 0, 2, pair_blocks(p), [block(0, 0, 2, b) for b in (0, 1)])
        for i, action in after_half.items():
            @pl.when(t == i)
            def _():
                action()

        return carry

    lax.fori_loop(0, 4, half_step, 0)

    sum_y(1)
    start(kv_y_last[1])
    start(kv_z[1])
    join_core(1)
    sum_y(2)
    start(dq_x[1])
    start(kv_z[2])
    sum_y_last(0)
    landed(core_in.at[0], core_sem.at[0])
    dq_acc[0, 0, :, :half] += core_in[0, :, :half]
    start(kv_z[3][:1])
    sum_y_last(1)
    dq_acc[0, 0, :, half:] += core_in[0, :, half:]
    start(kv_z[3][1:])
    for w in (0, 1):
        side = dq_acc[0, 0, :, w * half : (w + 1) * half]
        for i in (1, 0, 2):
            landed(x_in.at[i, w], x_sem.at[i, w])
            side = side + x_in[i, w].astype(F32)
        dq_rows[w] = jnp.transpose(side * scale)
    total = y_own[0, zhi]
    for i in (4, 1, 5, 3, 7):
        landed(z_in.at[i - 1], z_sem.at[i - 1])
        total = total + z_in[i - 1].astype(F32)
    dq_leave = pltpu.make_async_copy(dq_rows, dq_out.at[0], load_sem.at[0])
    dq_leave.start()
    for copy in sends:
        if all(copy is not last for last in kv_z[3]):
            copy.wait_send()
    for i in (2, 6):
        landed(z_in.at[i - 1], z_sem.at[i - 1])
        total = total + z_in[i - 1].astype(F32)
    dkv_out[0] = total[:, :feat] * scale
    dkv_out[1] = total[:, feat:]
    dq_leave.wait()
    for copy in kv_z[3]:
        copy.wait_send()


def finish(dq_in, dkv_in, dq_out, dk_out, dv_out, held, held_kv, in_sem, out_sem):
    half = held.shape[1]
    moves = [
        (dq_in.at[0, w], held.at[w], dq_out.at[0, pl.ds(w * half, half)]) for w in (0, 1)
    ] + [(dkv_in.at[i], held_kv.at[i], out) for i, out in enumerate((dk_out, dv_out))]
    arrivals = [
        pltpu.make_async_copy(src, at, in_sem.at[i]) for i, (src, at, _) in enumerate(moves)
    ]
    leaves = [
        pltpu.make_async_copy(at, dst, out_sem.at[i]) for i, (_, at, dst) in enumerate(moves)
    ]
    for copy in arrivals:
        copy.start()
    for arrival, leave in zip(arrivals, leaves):
        arrival.wait()
        leave.start()
    for leave in leaves:
        leave.wait()


def on_device(query, key, value, output, out_grad, lse, block_order):
    rows, feat = key.shape
    half, piece = rows // 2, rows // RING
    any_space = pl.BlockSpec(memory_space=pl.ANY)
    vmem = pl.BlockSpec(memory_space=pltpu.VMEM)
    dma = pltpu.SemaphoreType.DMA
    dq, dkv = pl.pallas_call(
        kernel,
        out_shape=(
            jax.ShapeDtypeStruct((1, 2, half, feat), F32),
            jax.ShapeDtypeStruct((2, piece, feat), F32),
        ),
        in_specs=[any_space] * 6 + [pl.BlockSpec(memory_space=pltpu.SMEM)],
        out_specs=(any_space, vmem),
        scratch_shapes=[
            pltpu.VMEM((4, 2 * rows, feat), BF16),
            pltpu.VMEM((4, 2 * rows, feat), BF16),
            pltpu.VMEM((4, 2, 2 * rows), F32),
            pltpu.VMEM((4, 2, Y, piece, feat), BF16),
            pltpu.VMEM((4, 2, Y, piece, feat), BF16),
            pltpu.VMEM((rows, feat), BF16),
            pltpu.VMEM((1, rows), F32),
            pltpu.VMEM((4, 2, feat, rows), F32),
            pltpu.VMEM((4, 2, Y, piece, feat), F32),
            pltpu.VMEM((4, 2, Y, piece, feat), F32),
            pltpu.VMEM((4, feat, rows), F32),
            pltpu.VMEM((3, 2, feat, half), BF16),
            pltpu.VMEM((3, 2, feat, half), BF16),
            pltpu.VMEM((4, Y, 2, piece, 2 * feat), BF16),
            pltpu.VMEM((4, 2, piece, 2 * feat), F32),
            pltpu.VMEM((4, Y - 1, 2, piece, 2 * feat), BF16),
            pltpu.VMEM((4, 2, piece, 2 * feat), BF16),
            pltpu.VMEM((RING - 1, piece, 2 * feat), BF16),
            pltpu.VMEM((2, half, feat), F32),
            dma((8,)),
            dma((80,)),
            dma((10,)),
            dma((10,)),
            dma((10,)),
            dma((4, 2)),
            dma((4, 2)),
            dma((4,)),
            dma((3, 2)),
            dma((5, Y - 1)),
            dma((RING - 1,)),
            pltpu.SemaphoreType.REGULAR((3,)),
        ],
        compiler_params=pltpu.CompilerParams(
            collective_id=0, has_side_effects=True, vmem_limit_bytes=67043328
        ),
        name="attention_backward",
    )(
        query,
        key.reshape(Y, 2, piece, feat),
        value.reshape(Y, 2, piece, feat),
        output, out_grad, lse, block_order,
    )
    return pl.pallas_call(
        finish,
        out_shape=(
            jax.ShapeDtypeStruct((1, rows, feat), F32),
            jax.ShapeDtypeStruct((piece, feat), F32),
            jax.ShapeDtypeStruct((piece, feat), F32),
        ),
        in_specs=[any_space] * 2,
        out_specs=(any_space,) * 3,
        scratch_shapes=[
            pltpu.VMEM((2, half, feat), F32),
            pltpu.VMEM((2, piece, feat), F32),
            dma((4,)),
            dma((4,)),
        ],
        compiler_params=pltpu.CompilerParams(vmem_limit_bytes=67043328),
        name="finish",
    )(dq, dkv)


def solution(mesh):
    in_specs = (
        P("head", "blk", None),
        P("blk", None),
        P("blk", None),
        P("head", "blk", None),
        P("head", "blk", None),
        P("head", "blk"),
        P(),
    )
    out_specs = (P("head", "blk", None), P(("blk", "head"), None), P(("blk", "head"), None))
    return jax.shard_map(
        on_device, mesh=mesh, in_specs=in_specs, out_specs=out_specs, check_vma=False
    )
```
